32 devices in a mesh: scene: 4 (over x, core), brick: 8 (over z, y).
Axes of the slice: x: 2, y: 2, z: 4, core: 2. Of those that a mesh axis runs over, the one named last changes fastest.
Arguments:
- features: bfloat16 [4, 4096, 64], P('scene', 'brick'), may hold values from -6 to 6
- cotangent: bfloat16 [4, 4096, 64], P('scene', 'brick'), may hold values from -6 to 6
- first_weight: bfloat16 [1728, 64], replicated, may hold values from -0.15625 to 0.15625
- second_weight: bfloat16 [1728, 64], replicated, may hold values from -0.15625 to 0.15625
- send_rows: int32 [4, 1024], P('scene', 'brick'), may hold values from 0 to 512, as said below
- gather_rows: int32 [4, 8000], P('scene', 'brick'), may hold values from 0 to 640, as said below
Outputs:
- output: bfloat16 [4, 4096, 64], P('scene', 'brick')
- grad_input: bfloat16 [4, 4096, 64], P('scene', 'brick')
- grad_first: float32 [1728, 64], replicated
- grad_second: float32 [1728, 64], replicated
The draws below stay inside these ranges and needn't reach their ends.
Inputs may be any that keep to these rules, and one draw needn't show every extreme that they name: `send_rows`: entries equal to 512 are empty slots; used entries come first in each half and name voxels on the face of active bricks towards that neighbour; in every draw some pair of neighbouring indices sends all 64 rows to each other. Index 0 sends nothing down, the last index nothing up. `gather_rows`: row 640 is the zero row; inactive slots read only it; rows 512 and up read boundary rows in the order of the neighbour's send list. Every index of brick holds exactly one active brick slot, and bricks touch only bricks of the same or an adjacent index.
All inputs are finite; a program needn't handle non-finite values.
Results may differ from the reference program's by a relative error of at most 0.0059.
Values may be sent and summed in bfloat16 or wider, within the bound.
No kernel may reach another device: no remote copies, remote signals or barrier semaphores. Data moves between devices by JAX's collectives and lax.ppermute only.
A program may use at most 64 MiB of HBM per device.

```python
import jax
import jax.numpy as jnp
from jax import lax

C = 64
EDGE = 8
B_CAP = 1
SIDE_Z = 2
VOX = 512
CAPV = 64
POOL = 641
PADDED = 1000
ROWS = 4096
N_SCENE = 4
N_BRICK = 8


def scene_tables(key):
    base = jax.random.fold_in(key, 1234)
    count_key, order_key, pair_key = jax.random.split(base, 3)
    scenes = N_SCENE
    devices = N_BRICK
    slots = B_CAP
    edge = EDGE
    side_y = 2
    places = side_y * SIDE_Z
    counts = jax.random.randint(count_key, (scenes, devices), (slots + 1) // 2, slots + 1)
    pair = jax.random.randint(pair_key, (scenes,), 0, devices - 1)
    device_ids = jnp.arange(devices)
    forced = (device_ids[None, :] == pair[:, None]) | (device_ids[None, :] == pair[:, None] + 1)
    counts = jnp.where(forced, slots, counts)
    scores = jax.random.randint(order_key, (scenes, devices, places), 0, 1 << 20) * places + jnp.arange(places)
    orders = jnp.argsort(scores, axis=-1).astype(jnp.int32)
    source = jnp.where(device_ids[None, :] == pair[:, None] + 1, pair[:, None], device_ids[None, :])
    orders = jnp.take_along_axis(orders, jnp.broadcast_to(source[:, :, None], (scenes, devices, places)), axis=1)
    position = orders[:, :, :slots]
    slot_ids = jnp.arange(slots)
    active = slot_ids[None, None, :] < counts[:, :, None]
    match = (position[..., None] == jnp.arange(places)) & active[..., None]
    slot_map = jnp.sum(jnp.where(match, slot_ids[None, None, :, None] + 1, 0), axis=2) - 1
    occupied = slot_map >= 0
    none_row = jnp.zeros((scenes, 1, places), bool)
    occupied_up = jnp.concatenate([occupied[:, 1:], none_row], axis=1)
    occupied_down = jnp.concatenate([none_row, occupied[:, :-1]], axis=1)
    pos_y = position // SIDE_Z
    pos_z = position % SIDE_Z
    place_y = jnp.arange(places) // SIDE_Z
    place_z = jnp.arange(places) % SIDE_Z
    inner = jnp.arange(edge)
    glob_y = pos_y[..., None] * edge + inner
    glob_z = pos_z[..., None] * edge + inner
    reach_y = (glob_y[..., None] >= place_y * edge - 1) & (glob_y[..., None] <= place_y * edge + edge)
    reach_z = (glob_z[..., None] >= place_z * edge - 1) & (glob_z[..., None] <= place_z * edge + edge)

    def side(occ_near, face):
        wanted = jnp.any(reach_y[:, :, :, :, None, :] & reach_z[:, :, :, None, :, :] & occ_near[:, :, None, None, None, :], axis=-1)
        wanted = wanted & active[:, :, :, None, None]
        flags = wanted.reshape(scenes, devices, CAPV).astype(jnp.int32)
        ranks = jnp.cumsum(flags, axis=-1) - 1
        candidate = (slot_ids[:, None, None] * edge ** 3 + face * edge * edge + inner[None, :, None] * edge + inner[None, None, :]).reshape(CAPV)
        order = jnp.argsort((1 - flags) * CAPV + jnp.arange(CAPV), axis=-1)
        chosen = candidate[order]
        used = jnp.arange(CAPV) < jnp.sum(flags, axis=-1, keepdims=True)
        return (jnp.where(used, chosen, VOX), ranks)
    rows_down, rank_down = side(occupied_down, 0)
    rows_up, rank_up = side(occupied_up, edge - 1)
    send = jnp.concatenate([rows_down, rows_up], axis=-1).reshape(scenes, devices * 2 * CAPV).astype(jnp.int32)
    span = jnp.arange(edge + 2)
    offset = jnp.where(span == 0, -1, jnp.where(span == edge + 1, 1, 0))
    within = span - 1 - offset * edge
    near_y = pos_y[..., None] + offset
    near_z = pos_z[..., None] + offset
    inside = ((near_y >= 0) & (near_y < side_y))[..., :, None] & ((near_z >= 0) & (near_z < SIDE_Z))[..., None, :]
    near_place = jnp.clip(near_y, 0, side_y - 1)[..., :, None] * SIDE_Z + jnp.clip(near_z, 0, SIDE_Z - 1)[..., None, :]
    flat_place = near_place.reshape(scenes, devices, -1)

    def lookup(map_near):
        return jnp.take_along_axis(map_near, flat_place, axis=2).reshape(near_place.shape)
    none_map = jnp.full((scenes, 1, places), -1, slot_map.dtype)
    map_up = jnp.concatenate([slot_map[:, 1:], none_map], axis=1)
    map_down = jnp.concatenate([none_map, slot_map[:, :-1]], axis=1)
    here = lookup(slot_map)
    above = lookup(map_up)
    below = lookup(map_down)
    face_index = within[:, None] * edge + within[None, :]
    zero_ranks = jnp.zeros((scenes, 1, CAPV), rank_down.dtype)
    ranks_above = jnp.concatenate([rank_down[:, 1:], zero_ranks], axis=1)
    ranks_below = jnp.concatenate([zero_ranks, rank_up[:, :-1]], axis=1)

    def rank_at(ranks_near, slot_near):
        index = jnp.maximum(slot_near, 0) * edge * edge + face_index
        return jnp.take_along_axis(ranks_near, index.reshape(scenes, devices, -1), axis=2).reshape(slot_near.shape)
    zero_row = POOL - 1
    from_above = jnp.where(inside & (above >= 0), VOX + CAPV + rank_at(ranks_above, above), zero_row)
    from_below = jnp.where(inside & (below >= 0), VOX + rank_at(ranks_below, below), zero_row)
    local_rows = jnp.maximum(here, 0)[:, :, :, None, :, :] * edge ** 3 + within[None, None, None, :, None, None] * edge * edge + face_index[None, None, None, None, :, :]
    pick_local = jnp.where((inside & (here >= 0))[:, :, :, None, :, :], local_rows, zero_row)
    step_x = offset[None, None, None, :, None, None]
    rows_all = jnp.where(step_x == 0, pick_local, jnp.where(step_x > 0, from_above[:, :, :, None, :, :], from_below[:, :, :, None, :, :]))
    rows_all = jnp.where(active[:, :, :, None, None, None], rows_all, zero_row)
    gather = rows_all.reshape(scenes, devices * slots * (edge + 2) ** 3).astype(jnp.int32)
    return (send, gather)


def draw_send_rows(key, part):
    return scene_tables(key)[0]


def draw_gather_rows(key, part):
    return scene_tables(key)[1]


def shard_levels(stream_key, extent, cuts, low, high):
    level, own = 1.0, jax.random.fold_in(stream_key, 6)
    for dim, parts in cuts:
        heights = jnp.exp(jax.random.uniform(jax.random.fold_in(own, dim), (parts,), jnp.float32, low / len(cuts), high / len(cuts)))
        level = level * jnp.repeat(heights, extent[dim] // parts).reshape([-1 if axis == dim else 1 for axis in range(len(extent))])
    return level


def centred(rng, shape, width, most, cuts=(), held_as=jnp.bfloat16):
    values = jax.random.normal(rng, shape, jnp.float32) * width
    if len(cuts) > 0:
        values = shard_levels(rng, shape, cuts, -0.22, 0.18) * values
    return jnp.clip(values, min=-most, max=most).astype(held_as)


def setup_inputs(seed: int = 0) -> dict:
    splits = jax.random.split(jax.random.key(seed), 7)
    return {
        "features": centred(splits[0], (N_SCENE, ROWS, C), 1.0, 6.0, ((0, 4), (1, 8))),
        "cotangent": centred(splits[1], (N_SCENE, ROWS, C), 1.0, 6.0, ((0, 4), (1, 8))),
        "first_weight": centred(splits[2], (27 * C, C), (27 * C) ** -0.5, 0.15625),
        "second_weight": centred(splits[3], (27 * C, C), (27 * C) ** -0.5, 0.15625),
        "send_rows": draw_send_rows(jax.random.fold_in(splits[6], 71), 0),
        "gather_rows": draw_gather_rows(jax.random.fold_in(splits[6], 71), 0),
    }


def silu_slope(values):
    sig = jax.nn.sigmoid(values)
    return sig * (1.0 + values * (1.0 - sig))


def scene_padded(values, send_list, gather_list):
    blocks = values.reshape(N_BRICK, VOX, C)
    zero_rows = jnp.zeros((N_BRICK, 1, C), values.dtype)
    extended = jnp.concatenate([blocks, zero_rows], axis=1)
    sent = jax.vmap(lambda rows, index: jnp.take(rows, index, axis=0))(extended, send_list.reshape(N_BRICK, 2 * CAPV))
    empty = jnp.zeros((1, CAPV, C), values.dtype)
    from_lower = jnp.concatenate([empty, sent[:-1, CAPV:]], axis=0)
    from_upper = jnp.concatenate([sent[1:, :CAPV], empty], axis=0)
    pool = jnp.concatenate([blocks, from_lower, from_upper, zero_rows], axis=1)
    padded = jax.vmap(lambda rows, index: jnp.take(rows, index, axis=0))(pool, gather_list.reshape(N_BRICK, B_CAP * PADDED))
    return padded.reshape(N_BRICK * B_CAP, EDGE + 2, EDGE + 2, EDGE + 2, C)


def window_rows(padded, row_off, col_off):
    slabs = [padded[:, row_off:row_off + EDGE, col_off:col_off + EDGE, depth:depth + EDGE, :] for depth in range(3)]
    return jnp.concatenate(slabs, axis=-1).reshape(-1, 3 * C)


def convolve(padded, weight):
    accumulated = jnp.zeros((padded.shape[0] * EDGE ** 3, weight.shape[1]), jnp.float32)
    for row_off in range(3):
        for col_off in range(3):
            start = (row_off * 3 + col_off) * 3 * C
            accumulated = accumulated + jnp.dot(window_rows(padded, row_off, col_off), weight[start:start + 3 * C], preferred_element_type=jnp.float32)
    return accumulated


def weight_gradient(padded, delta_rows):
    pieces = []
    for row_off in range(3):
        for col_off in range(3):
            pieces.append(lax.dot_general(window_rows(padded, row_off, col_off), delta_rows, (((0,), (0,)), ((), ())), preferred_element_type=jnp.float32))
    return jnp.concatenate(pieces, axis=0)


def flipped(weight):
    return jnp.transpose(weight.reshape(27, C, C)[::-1], (0, 2, 1)).reshape(27 * C, C)


def one_scene(items):
    values, cot_rows, send_list, gather_list, first_weight, second_weight = items
    padded_input = scene_padded(values, send_list, gather_list)
    first_pre = convolve(padded_input, first_weight)
    first_act = (first_pre * jax.nn.sigmoid(first_pre)).astype(jnp.bfloat16)
    padded_act = scene_padded(first_act, send_list, gather_list)
    second_pre = convolve(padded_act, second_weight)
    output = (second_pre * jax.nn.sigmoid(second_pre)).astype(jnp.bfloat16)
    second_delta = (cot_rows.astype(jnp.float32) * silu_slope(second_pre)).astype(jnp.bfloat16)
    grad_second = weight_gradient(padded_act, second_delta)
    first_back = convolve(scene_padded(second_delta, send_list, gather_list), flipped(second_weight))
    first_delta = (first_back * silu_slope(first_pre)).astype(jnp.bfloat16)
    grad_first = weight_gradient(padded_input, first_delta)
    grad_input = convolve(scene_padded(first_delta, send_list, gather_list), flipped(first_weight)).astype(jnp.bfloat16)
    return output, grad_input, grad_first, grad_second


def reference(features, cotangent, first_weight, second_weight, send_rows, gather_rows):
    def step(items):
        return one_scene((items[0], items[1], items[2], items[3], first_weight, second_weight))

    output, grad_input, grad_first, grad_second = lax.map(step, (features, cotangent, send_rows, gather_rows))
    factor = float(N_SCENE * N_BRICK * VOX) ** -0.5
    return output, grad_input, jnp.sum(grad_first, axis=0) * factor, jnp.sum(grad_second, axis=0) * factor
```

```python
import jax
import jax.numpy as jnp
from jax import lax
from jax.experimental import pallas as pl
from jax.experimental.pallas import tpu as pltpu
from jax.sharding import PartitionSpec as P

F32 = jnp.float32
BF16 = jnp.bfloat16

E = 8
C = 64
FACE = E * E
VOX = E * FACE
RIM = E + 2
CELLS = 3 * RIM * E
BOTH = ("scene", "brick")

PAIRS = (
    ((0, 0), (0, 1)),
    ((1, 0), (1, 1)),
    ((2, 0), (2, 1)),
    ((0, 2), (1, 2)),
    ((2, 2), None),
)
TILES = len(PAIRS)
KDIM = TILES * 2 * C
VMEM_SPEC = pl.BlockSpec(memory_space=pltpu.VMEM)
SMEM_SPEC = pl.BlockSpec(memory_space=pltpu.SMEM)


def sigmoid(v):
    return jax.nn.sigmoid(v)


def slope(v):
    s = sigmoid(v)
    return s * (1.0 + v * (1.0 - s))


def low_lanes(shape):
    return lax.broadcasted_iota(jnp.int32, shape, len(shape) - 1) % (2 * C) < C


def twice(v):
    return jnp.concatenate([v, v], axis=-1)


def weight_kernel(w1_ref, w2_ref, f1_ref, f2_ref, b1_ref, b2_ref):
    zero = jnp.zeros((C, C), BF16)
    for w_ref, f_ref, b_ref in ((w1_ref, f1_ref, b1_ref), (w2_ref, f2_ref, b2_ref)):
        blocks = [w_ref[o * C : (o + 1) * C, :] for o in range(27)]
        for t, pair in enumerate(PAIRS):
            for h, bc in enumerate(pair):
                rows = slice((2 * t + h) * C, (2 * t + h + 1) * C)
                if bc is None:
                    f_ref[rows, :] = jnp.zeros((C, 4 * C), BF16)
                    continue
                o = 3 * bc[0] + bc[1]
                f_ref[rows, 0 : 2 * C] = jnp.concatenate([blocks[o], blocks[9 + o]], axis=1)
                f_ref[rows, 2 * C : 4 * C] = jnp.concatenate([blocks[18 + o], blocks[18 + o]], axis=1)
            for k, a in enumerate((0, 1, 2, 2)):
                halves = [
                    zero if bc is None else blocks[26 - (9 * a + 3 * bc[0] + bc[1])] for bc in pair
                ]
                b_ref[k * C : (k + 1) * C, t * 2 * C : (t + 1) * 2 * C] = jnp.concatenate(halves, axis=1)


def prepare_weights(w1, w2):
    fwd = jax.ShapeDtypeStruct((KDIM, 4 * C), BF16)
    bwd = jax.ShapeDtypeStruct((4 * C, KDIM), BF16)
    return pl.pallas_call(
        weight_kernel,
        out_shape=(fwd, fwd, bwd, bwd),
        in_specs=[VMEM_SPEC] * 2,
        out_specs=(VMEM_SPEC,) * 4,
        cost_estimate=pl.CostEstimate(flops=0, bytes_accessed=2 << 20, transcendentals=0),
    )(w1, w2)


def z_shifted(v):
    axis = v.ndim - 2
    z = lax.broadcasted_iota(jnp.int32, v.shape, axis)
    before = jnp.where(z == 0, 0.0, pltpu.roll(v, 1, axis))
    after = jnp.where(z == E - 1, 0.0, pltpu.roll(v, E - 1, axis))
    return jnp.where(low_lanes(v.shape), before, v), after


def rim_cells(pick, plane):
    m = jnp.dot(pick, plane.reshape(FACE, 2 * C).astype(BF16), preferred_element_type=F32)
    m = m.reshape(3, RIM, E, 2 * C)
    return jnp.where(low_lanes(m.shape[1:]), m[0], m[1]), m[2]


def pick_matrix(send_codes, cell_codes):
    row = lax.broadcasted_iota(jnp.int32, (FACE, 2 * C), 0).astype(F32) + 1.0
    listed = jnp.where(row == send_codes, 1.0, 0.0).astype(BF16)
    slot = lax.broadcasted_iota(jnp.int32, (2 * C, 4 * C), 0).astype(F32) + 1.0
    cells = jnp.concatenate([cell_codes[0:1], cell_codes[1:2]], axis=1)
    read = jnp.where(slot == cells, 1.0, 0.0).astype(BF16)
    picked = jnp.dot(listed, read, preferred_element_type=F32)
    return jnp.transpose(picked)[:CELLS].astype(BF16)


def stack_x(planes):
    count = planes.shape[0] // E
    v = planes.reshape(count, E, E, 2 * C)
    return jnp.stack([v[:, y] for y in range(E)], axis=0)


def x_taps(r, first, count):
    here = slice(first, first + count)
    prev = slice(first - 1, first + count - 1)
    after = slice(first + 1, first + count + 1)
    v0 = r[..., : 2 * C]
    v1 = r[..., 2 * C :]
    s = jnp.where(low_lanes((E, count, E, 2 * C)), v0[:, prev], v0[:, here])
    return s + pltpu.roll(s, C, 3) + v1[:, after]


def put_interior(q_ref, first, v):
    count = v.shape[1]
    rows = pl.ds(first * E, count * E)
    z0, z1 = z_shifted(v)
    z0 = z0.reshape(E, count * E, 2 * C).astype(BF16)
    zero = jnp.zeros((1, count, E, 2 * C), F32)
    pair = jnp.where(low_lanes(v.shape), jnp.concatenate([zero, z1[: E - 1]], axis=0), z1)
    pair = pair.reshape(E, count * E, 2 * C).astype(BF16)
    z1 = z1.reshape(E, count * E, 2 * C).astype(BF16)
    none = jnp.zeros((count * E, 2 * C), BF16)
    for y in range(E):
        q_ref[y, rows, 0 : 2 * C] = z0[y - 1] if y > 0 else none
        q_ref[y, rows, 2 * C : 4 * C] = z0[y]
        q_ref[y, rows, 4 * C : 6 * C] = z0[y + 1] if y < E - 1 else none
        q_ref[y, rows, 6 * C : 8 * C] = pair[y]
        q_ref[y, rows, 8 * C : 10 * C] = z1[y + 1] if y < E - 1 else none


def put_rims(q_ref, first, rims):
    count = len(rims)
    rows = pl.ds(first * E, count * E)
    z0 = jnp.stack([r[0] for r in rims], axis=1)
    z1 = jnp.stack([r[1] for r in rims], axis=1)
    pair = jnp.where(low_lanes(z1[:-1].shape), z1[:-1], z1[1:])
    z0 = z0.reshape(RIM, count * E, 2 * C).astype(BF16)
    z1 = z1.reshape(RIM, count * E, 2 * C).astype(BF16)
    pair = pair.reshape(RIM - 1, count * E, 2 * C).astype(BF16)
    for y in range(E):
        for b in range(3):
            q_ref[y, rows, b * 2 * C : (b + 1) * 2 * C] = z0[y + b]
        q_ref[y, rows, 6 * C : 8 * C] = pair[y]
        q_ref[y, rows, 8 * C : 10 * C] = z1[y + 2]


LOW, OWN, HIGH = 0, 6, 16
PLANES = 20
WIDE = 4
SPAN = 2


def fill(q_ref, low, own, high, picks):
    low_pick, below_pick, above_pick, high_pick = picks
    put_interior(q_ref, OWN, own)
    put_interior(q_ref, LOW, low)
    put_interior(q_ref, HIGH, high)
    put_rims(
        q_ref,
        OWN - 2,
        [rim_cells(low_pick, own[:, 0]), rim_cells(below_pick, low[:, -1])],
    )
    put_rims(
        q_ref,
        OWN + E,
        [rim_cells(above_pick, high[:, 0]), rim_cells(high_pick, own[:, -1])],
    )


def main_kernel(
    even_ref,
    feat_ref,
    cot_ref,
    first_ref,
    second_ref,
    down_codes_ref,
    up_codes_ref,
    f1_ref,
    f2_ref,
    b2_ref,
    out_ref,
    grad_ref,
    delta_ref,
    pick_ref,
    q1_ref,
    q2_ref,
    q3_ref,
):
    even = even_ref[0] == 1
    first = first_ref[...]
    second = second_ref[...]
    upper = jnp.where(even, first, second).astype(F32)
    lower = jnp.where(even, second, first).astype(F32)

    half = WIDE * FACE // 2
    quarter = SPAN * FACE // 2
    lanes_low = low_lanes((half, 2 * C))

    def both_halves(packed):
        n = packed.shape[0]
        keep = low_lanes(packed.shape)
        turned = pltpu.roll(packed, C, 1)
        return jnp.concatenate(
            [jnp.where(keep, packed, turned), jnp.where(keep, turned, packed)], axis=0
        ).reshape(2 * n // E, E, 2 * C)

    def parts(packed):
        f = stack_x(both_halves(packed[:half]))
        c = stack_x(both_halves(packed[half : half + quarter]))
        codes = packed[half + quarter : half + quarter + 8]
        return f, c, codes[0:1], codes[1:3]

    low_f, low_c, low_send, low_cells = parts(lower)
    high_f, high_c, high_send, high_cells = parts(upper)
    down_codes = down_codes_ref[...].astype(F32)
    up_codes = up_codes_ref[...].astype(F32)
    own_f = stack_x(twice(feat_ref[0].astype(F32)).reshape(FACE, E, 2 * C))
    own_c = stack_x(twice(cot_ref[0].astype(F32)).reshape(FACE, E, 2 * C))

    picks = (
        pick_matrix(down_codes[0:1], low_cells),
        pick_matrix(low_send, down_codes[1:3]),
        pick_matrix(high_send, up_codes[1:3]),
        pick_matrix(up_codes[0:1], high_cells),
    )
    pick_ref[0] = picks[1]
    pick_ref[1] = picks[2]

    def conv(q_ref, w, flipped=False):
        q = q_ref[...].reshape(E * PLANES * E, KDIM)
        dims = (((1,), (1 if flipped else 0,)), ((), ()))
        r = lax.dot_general(q, w, dims, preferred_element_type=F32)
        return r.reshape(E, PLANES, E, 4 * C)

    def rounded(v):
        return v.astype(BF16).astype(F32)

    def weight_gradient(which, q_ref, delta):
        zero = jnp.zeros((E, 1, E, 2 * C), F32)
        d = jnp.concatenate([zero, zero, delta, zero, zero, zero], axis=1)
        n = E + 4
        before = jnp.concatenate([zero, d[:, : n - 1]], axis=1)
        d0 = jnp.where(low_lanes((E, n, E, 2 * C)), d[:, 1 : n + 1], d[:, :n])
        d1 = before
        rows = E * n * E
        d0 = jnp.transpose(d0.reshape(rows, 2 * C)).astype(BF16)
        d1 = jnp.transpose(d1.reshape(rows, 2 * C))[:C].astype(BF16)
        dt = jnp.concatenate([d0, d1], axis=0)
        q = q_ref[:, (OWN - 2) * E : (OWN + E + 2) * E, :].reshape(rows, KDIM)
        g = jnp.dot(dt, q, preferred_element_type=F32).astype(BF16)
        for t in range(TILES):
            grad_ref[which, t] = g[:, t * 2 * C : (t + 1) * 2 * C]

    fill(q1_ref, low_f, own_f, high_f, picks)
    r = conv(q1_ref, f1_ref[...])
    pre_low = x_taps(r, LOW + 1, WIDE - 1)
    pre_own = x_taps(r, OWN, E)
    pre_high = x_taps(r, HIGH, WIDE - 1)
    act = [rounded(v * sigmoid(v)) for v in (pre_low, pre_own, pre_high)]
    pad_plane = jnp.zeros((E, 1, E, 2 * C), F32)
    fill(
        q2_ref,
        jnp.concatenate([pad_plane, act[0]], axis=1),
        act[1],
        jnp.concatenate([act[2], pad_plane], axis=1),
        picks,
    )
    r = conv(q2_ref, f2_ref[...])
    second_own = x_taps(r, OWN, E)
    out = (second_own * sigmoid(second_own))[..., :C]
    for y in range(E):
        for x in range(E):
            out_ref[0, x * FACE + y * E : x * FACE + (y + 1) * E, :] = out[y, x].astype(BF16)
    second_low = x_taps(r, LOW + WIDE - SPAN, SPAN)
    second_high = x_taps(r, HIGH, SPAN)
    delta_own = rounded(own_c * slope(second_own))
    delta_low = rounded(low_c * slope(second_low))
    delta_high = rounded(high_c * slope(second_high))
    weight_gradient(1, q2_ref, delta_own)
    pads = jnp.zeros((E, WIDE - SPAN, E, 2 * C), F32)
    fill(
        q3_ref,
        jnp.concatenate([pads, delta_low], axis=1),
        delta_own,
        jnp.concatenate([delta_high, pads], axis=1),
        picks,
    )
    r = conv(q3_ref, b2_ref[...], True)
    first_own = rounded(x_taps(r, OWN, E) * slope(pre_own))
    first_low = rounded(x_taps(r, LOW + WIDE - 1, 1) * slope(pre_low[:, -1:]))
    first_high = rounded(x_taps(r, HIGH, 1) * slope(pre_high[:, :1]))
    weight_gradient(0, q1_ref, first_own)
    delta = jnp.concatenate([first_low, first_own, first_high], axis=1)
    delta_ref[...] = delta.reshape(E, (E + 2) * E, 2 * C).astype(BF16)


def main_call(even, feat, cot, first, second, down_codes, up_codes, f1, f2, b2):
    q_shape = pltpu.VMEM((E, PLANES * E, KDIM), BF16)
    return pl.pallas_call(
        main_kernel,
        out_shape=(
            jax.ShapeDtypeStruct(feat.shape, BF16),
            jax.ShapeDtypeStruct((2, TILES, 3 * C, 2 * C), BF16),
            jax.ShapeDtypeStruct((E, (E + 2) * E, 2 * C), BF16),
            jax.ShapeDtypeStruct((2, CELLS, FACE), BF16),
        ),
        in_specs=[SMEM_SPEC] + [VMEM_SPEC] * 9,
        out_specs=(VMEM_SPEC,) * 4,
        scratch_shapes=[q_shape] * 3,
        cost_estimate=pl.CostEstimate(flops=10**10, bytes_accessed=4 << 20, transcendentals=10**6),
    )(even, feat, cot, first, second, down_codes, up_codes, f1, f2, b2)


def last_kernel(delta_ref, pick_ref, b1_ref, out_ref, q_ref):
    delta = delta_ref[...].astype(F32).reshape(E, E + 2, E, 2 * C)
    put_interior(q_ref, 2, delta[:, 1 : E + 1])
    below = rim_cells(pick_ref[0], delta[:, 0])
    above = rim_cells(pick_ref[1], delta[:, E + 1])
    put_rims(q_ref, 0, [below, below])
    put_rims(q_ref, E + 2, [above, above])
    q = q_ref[...].reshape(E * (E + 4) * E, KDIM)
    r = lax.dot_general(q, b1_ref[...], (((1,), (1,)), ((), ())), preferred_element_type=F32)
    out = x_taps(r.reshape(E, E + 4, E, 4 * C), 2, E)[..., :C]
    for y in range(E):
        for x in range(E):
            out_ref[0, x * FACE + y * E : x * FACE + (y + 1) * E, :] = out[y, x].astype(BF16)


def last_call(delta, pick, b1, shape):
    return pl.pallas_call(
        last_kernel,
        out_shape=jax.ShapeDtypeStruct(shape, BF16),
        in_specs=[VMEM_SPEC] * 3,
        out_specs=VMEM_SPEC,
        scratch_shapes=[pltpu.VMEM((E, (E + 4) * E, KDIM), BF16)],
        cost_estimate=pl.CostEstimate(flops=10**9, bytes_accessed=2 << 20, transcendentals=0),
    )(delta, pick, b1)


def finish_kernel(scale, total_ref, g1_ref, g2_ref):
    for which, g_ref in ((0, g1_ref), (1, g2_ref)):
        for t, pair in enumerate(PAIRS):
            turned = jnp.transpose(total_ref[which, t].astype(F32)) * scale
            for h, bc in enumerate(pair):
                if bc is None:
                    continue
                for a in range(3):
                    o = 9 * a + 3 * bc[0] + bc[1]
                    g_ref[o * C : (o + 1) * C, :] = turned[h * C : (h + 1) * C, a * C : (a + 1) * C]


def finish(total, scale):
    shape = jax.ShapeDtypeStruct((27 * C, C), F32)
    return pl.pallas_call(
        lambda *refs: finish_kernel(scale, *refs),
        out_shape=(shape, shape),
        in_specs=[VMEM_SPEC],
        out_specs=(VMEM_SPEC,) * 2,
    )(total)


def xor_permute(v, scene_bits, brick_bits):
    bricks = lax.axis_size("brick")
    total = lax.axis_size("scene") * bricks
    pairs = [
        (i, ((i // bricks) ^ scene_bits) * bricks + ((i % bricks) ^ brick_bits)) for i in range(total)
    ]
    return lax.ppermute(v, BOTH, pairs)


def all_sum(v):
    scenes, bricks = lax.axis_size("scene"), lax.axis_size("brick")
    if scenes != 4 or bricks != 8:
        return lax.psum(v.astype(F32), BOTH)
    shape = v.shape
    scene, brick = lax.axis_index("scene"), lax.axis_index("brick")
    core, across = scene & 1, scene >> 1
    where = across * 2 + (brick & 1)
    parts = v.reshape(2, 4, -1, 2 * C)

    def pick(array, index):
        return lax.dynamic_index_in_dim(array, index, 0, keepdims=False)

    def sum4(own, one, two, three):
        return (own.astype(F32) + one.astype(F32)) + (two.astype(F32) + three.astype(F32))

    other = xor_permute(pick(parts, 1 - core), 1, 0)
    chip = (pick(parts, core).astype(F32) + other.astype(F32)).astype(BF16)
    moved = [
        xor_permute(pick(chip, where ^ k), 2 * (k >> 1), k & 1) for k in (1, 2, 3)
    ]
    plane = sum4(pick(chip, where), *moved).astype(BF16)
    column = [xor_permute(plane, 0, 2 * k) for k in (1, 2, 3)]
    whole = sum4(plane, *column).astype(BF16)
    back = [xor_permute(whole, 2 * (k >> 1), k & 1) for k in (1, 2, 3)]
    mine = jnp.zeros(chip.shape, BF16)
    for k, piece in enumerate([whole] + back):
        mine = lax.dynamic_update_index_in_dim(mine, piece, where ^ k, 0)
    theirs = xor_permute(mine, 1, 0)
    full = jnp.where(core == 0, jnp.stack([mine, theirs]), jnp.stack([theirs, mine]))
    return full.reshape(shape)


def rim_codes(send_half, plane, face_start, pool_start):
    row = send_half - face_start
    sent = jnp.where((row >= 0) & (row < FACE), row + 1, 0)
    sent = jnp.pad(sent, (0, 2 * C - sent.shape[0]))
    slot = plane.reshape(RIM, RIM) - pool_start
    slot = jnp.where((slot >= 0) & (slot < FACE), slot + 1, 0)
    cells = jnp.stack([slot[:, c : c + E] for c in range(3)]).reshape(-1)
    cells = jnp.pad(cells, (0, 4 * C - CELLS)).reshape(2, 2 * C)
    codes = jnp.concatenate([sent[None], cells], axis=0)
    return jnp.pad(codes, ((0, 5), (0, 0))).astype(BF16)


def lane_pairs(rows):
    n = rows.shape[0] // 2
    return jnp.concatenate([rows[:n], rows[n:]], axis=1)


def shards(features, cotangent, first_weight, second_weight, send_rows, gather_rows):
    bricks = lax.axis_size("brick")
    feat, cot = features[0], cotangent[0]
    send, gather = send_rows[0], gather_rows[0]
    even = (lax.axis_index("brick") & 1) == 0

    down_codes = rim_codes(send[:FACE], gather[: RIM * RIM], 0, VOX)
    up_codes = rim_codes(send[FACE:], gather[-RIM * RIM :], VOX - FACE, VOX + FACE)
    down = jnp.concatenate(
        [lane_pairs(feat[: WIDE * FACE]), lane_pairs(cot[: SPAN * FACE]), down_codes], axis=0
    )
    up = jnp.concatenate(
        [lane_pairs(feat[-WIDE * FACE :]), lane_pairs(cot[-SPAN * FACE :]), up_codes], axis=0
    )
    within = [(i, i ^ 1) for i in range(bricks) if i ^ 1 < bricks]
    between = [(i, ((i + 1) ^ 1) - 1) for i in range(1, bricks) if ((i + 1) ^ 1) - 1 < bricks]
    first = lax.ppermute(jnp.where(even, up, down), "brick", within)
    second = lax.ppermute(jnp.where(even, down, up), "brick", between)
    f1, f2, b1, b2 = prepare_weights(first_weight, second_weight)

    output, grads, delta, pick = main_call(
        even.astype(jnp.int32)[None], features, cotangent, first, second, down_codes, up_codes, f1, f2, b2
    )
    grad_input = last_call(delta, pick, b1, features.shape)
    total = all_sum(grads)
    scale = float(lax.axis_size("scene") * bricks * features.shape[1]) ** -0.5
    grad_first, grad_second = finish(total, scale)
    return output, grad_input, grad_first, grad_second


def solution(mesh):
    rows = P("scene", "brick", None)
    table = P("scene", "brick")
    return jax.shard_map(
        shards,
        mesh=mesh,
        in_specs=(rows, rows, P(), P(), table, table),
        out_specs=(rows, rows, P(), P()),
        check_vma=False,
    )
```

```python
import jax
import jax.numpy as jnp
from jax import lax
from jax.experimental import pallas as pl
from jax.experimental.pallas import tpu as pltpu
from jax.sharding import PartitionSpec as P

F32 = jnp.float32
BF16 = jnp.bfloat16

E = 8
C = 64
FACE = E * E
VOX = E * FACE
RIM = E + 2
CELLS = 3 * RIM * E
BOTH = ("scene", "brick")

PAIRS = (
    ((0, 0), (0, 1)),
    ((1, 0), (1, 1)),
    ((2, 0), (2, 1)),
    ((0, 2), (1, 2)),
    ((2, 2), None),
)
TILES = len(PAIRS)
KDIM = TILES * 2 * C
LOW, OWN, HIGH = 0, 6, 16
PLANES = 20
WIDE = 4
SPAN = 2

LIMIT = pltpu.CompilerParams(vmem_limit_bytes=24 << 20)
VMEM_SPEC = pl.BlockSpec(memory_space=pltpu.VMEM)
SMEM_SPEC = pl.BlockSpec(memory_space=pltpu.SMEM)


def sigmoid(v):
    return jax.nn.sigmoid(v)


def slope(v):
    s = sigmoid(v)
    return s * (1.0 + v * (1.0 - s))


def low_lanes(shape):
    return lax.broadcasted_iota(jnp.int32, shape, len(shape) - 1) % (2 * C) < C


def weight_kernel(w1_ref, w2_ref, f1_ref, f2_ref, b1_ref, b2_ref):
    zero = jnp.zeros((C, C), BF16)
    for w_ref, f_ref, b_ref in ((w1_ref, f1_ref, b1_ref), (w2_ref, f2_ref, b2_ref)):
        blocks = [w_ref[:, o * C : (o + 1) * C] for o in range(27)]
        for t, pair in enumerate(PAIRS):
            for k, a in enumerate((0, 1, 2, 2)):
                halves = [zero if bc is None else blocks[9 * a + 3 * bc[0] + bc[1]] for bc in pair]
                f_ref[k * C : (k + 1) * C, t * 2 * C : (t + 1) * 2 * C] = jnp.concatenate(halves, axis=1)
            for h, bc in enumerate(pair):
                rows = slice((2 * t + h) * C, (2 * t + h + 1) * C)
                if bc is None:
                    b_ref[rows, :] = jnp.zeros((C, 4 * C), BF16)
                    continue
                o = 26 - 3 * bc[0] - bc[1]
                b_ref[rows, 0 : 2 * C] = jnp.concatenate([blocks[o], blocks[o - 9]], axis=1)
                b_ref[rows, 2 * C : 4 * C] = jnp.concatenate([blocks[o - 18], blocks[o - 18]], axis=1)


def prepare_weights(w1, w2):
    fwd = jax.ShapeDtypeStruct((4 * C, KDIM), BF16)
    bwd = jax.ShapeDtypeStruct((KDIM, 4 * C), BF16)
    return pl.pallas_call(
        weight_kernel,
        out_shape=(fwd, fwd, bwd, bwd),
        in_specs=[VMEM_SPEC] * 2,
        out_specs=(VMEM_SPEC,) * 4,
        compiler_params=LIMIT,
        cost_estimate=pl.CostEstimate(flops=0, bytes_accessed=2 << 20, transcendentals=0),
    )(w1, w2)


def rim_spread(first):
    lane = lax.broadcasted_iota(jnp.int32, (2 * C, 4 * C), 1)
    c = jnp.where(lane >= RIM * E, 1, 0) + jnp.where(lane >= 2 * RIM * E, 1, 0)
    cell = lane - c * (RIM * E)
    source = (cell >> 3) * RIM + (cell & (E - 1)) + c + first
    return jnp.where(lax.broadcasted_iota(jnp.int32, (2 * C, 4 * C), 0) == source, 1.0, 0.0).astype(BF16)


def pack_kernel(even_ref, feat_ref, cot_ref, send_ref, gather_ref, first_ref, second_ref, codes_ref):
    send = send_ref[...]
    upper = lax.broadcasted_iota(jnp.int32, send.shape, 1) >= FACE
    row = jnp.where(upper, send - (VOX - FACE), send)
    sent = jnp.where((row >= 0) & (row < FACE), row + 1, 0)
    slot = gather_ref[:, : 2 * C] - VOX
    bottom = jnp.where((slot >= 0) & (slot < FACE), slot + FACE + 1, 0)
    slot = gather_ref[:, -2 * C :] - (VOX + FACE)
    top = jnp.where((slot >= 0) & (slot < FACE), slot + 1, 0)

    def spread(cells, first):
        wide = jnp.broadcast_to(cells.astype(F32), (E, 2 * C)).astype(BF16)
        v = jnp.dot(wide, rim_spread(first), preferred_element_type=F32)
        return [v[:1, : 2 * C], v[:1, 2 * C :]]

    rows = [sent.astype(F32)] + spread(bottom, 0) + spread(top, 2 * C - RIM * RIM)
    codes = jnp.concatenate(rows + [jnp.zeros((E - len(rows), 2 * C), F32)], axis=0).astype(BF16)
    codes_ref[...] = codes
    even = even_ref[0] == 1

    def put(ref, upward):
        at = 0
        for source, layers in ((feat_ref, WIDE), (cot_ref, SPAN)):
            start = VOX - layers * FACE if upward else 0
            for lane in range(start, start + layers * FACE, 2 * C):
                ref[at : at + C, :] = source[0, :, lane : lane + 2 * C]
                at += C
        ref[at : at + E, :] = codes

    @pl.when(even)
    def _():
        put(first_ref, True)
        put(second_ref, False)

    @pl.when(jnp.logical_not(even))
    def _():
        put(first_ref, False)
        put(second_ref, True)


def pack(even, feat, cot, send, gather):
    rows = (WIDE + SPAN) * FACE * C // (2 * C) + E
    return pl.pallas_call(
        pack_kernel,
        out_shape=(jax.ShapeDtypeStruct((rows, 2 * C), BF16),) * 2
        + (jax.ShapeDtypeStruct((E, 2 * C), BF16),),
        in_specs=[SMEM_SPEC] + [VMEM_SPEC] * 4,
        out_specs=(VMEM_SPEC,) * 3,
        compiler_params=LIMIT,
    )(even, feat, cot, send, gather)


def z_shifted(v):
    axis = v.ndim - 2
    z = lax.broadcasted_iota(jnp.int32, v.shape, axis)
    before = jnp.where(z == 0, 0.0, pltpu.roll(v, 1, axis))
    after = jnp.where(z == E - 1, 0.0, pltpu.roll(v, E - 1, axis))
    return jnp.where(low_lanes(v.shape), before, v), after


def rim_cells(pick, plane):
    m = jnp.dot(pick, plane.reshape(FACE, 2 * C).astype(BF16), preferred_element_type=F32)
    m = m.reshape(3, RIM, E, 2 * C)
    return jnp.where(low_lanes(m.shape[1:]), m[0], m[1]), m[2]


def pick_matrix(send_codes, cell_codes):
    row = lax.broadcasted_iota(jnp.int32, (FACE, 2 * C), 0).astype(F32) + 1.0
    listed = jnp.where(row == send_codes, 1.0, 0.0).astype(BF16)
    slot = lax.broadcasted_iota(jnp.int32, (2 * C, 4 * C), 0).astype(F32) + 1.0
    cells = jnp.concatenate([cell_codes[0:1], cell_codes[1:2]], axis=1)
    read = jnp.where(slot == cells, 1.0, 0.0).astype(BF16)
    picked = jnp.dot(listed, read, preferred_element_type=F32)
    return jnp.transpose(picked)[:CELLS].astype(BF16)


def stack_x(planes):
    count = planes.shape[0] // E
    v = planes.reshape(count, E, E, 2 * C)
    return jnp.stack([v[:, y] for y in range(E)], axis=0)


def x_taps(r, first, count):
    here = slice(first, first + count)
    prev = slice(first - 1, first + count - 1)
    after = slice(first + 1, first + count + 1)
    v0 = r[..., : 2 * C]
    v1 = r[..., 2 * C :]
    s = jnp.where(low_lanes((E, count, E, 2 * C)), v0[:, prev], v0[:, here])
    return s + pltpu.roll(s, C, 3) + v1[:, after]


def put_rows(out_ref, v):
    rows = jnp.stack([v[:, x] for x in range(E)], axis=0).reshape(VOX, 2 * C)
    out_ref[0] = jnp.transpose(rows)[:C].astype(BF16)


def put_interior(q_ref, first, v):
    count = v.shape[1]
    rows = pl.ds(first * E, count * E)
    z0, z1 = z_shifted(v)
    z0 = z0.reshape(E, count * E, 2 * C).astype(BF16)
    zero = jnp.zeros((1, count, E, 2 * C), F32)
    pair = jnp.where(low_lanes(v.shape), jnp.concatenate([zero, z1[: E - 1]], axis=0), z1)
    pair = pair.reshape(E, count * E, 2 * C).astype(BF16)
    z1 = z1.reshape(E, count * E, 2 * C).astype(BF16)
    none = jnp.zeros((count * E, 2 * C), BF16)
    for y in range(E):
        q_ref[y, rows, 0 : 2 * C] = z0[y - 1] if y > 0 else none
        q_ref[y, rows, 2 * C : 4 * C] = z0[y]
        q_ref[y, rows, 4 * C : 6 * C] = z0[y + 1] if y < E - 1 else none
        q_ref[y, rows, 6 * C : 8 * C] = pair[y]
        q_ref[y, rows, 8 * C : 10 * C] = z1[y + 1] if y < E - 1 else none


def put_rims(q_ref, first, rims):
    count = len(rims)
    rows = pl.ds(first * E, count * E)
    z0 = jnp.stack([r[0] for r in rims], axis=1)
    z1 = jnp.stack([r[1] for r in rims], axis=1)
    pair = jnp.where(low_lanes(z1[:-1].shape), z1[:-1], z1[1:])
    z0 = z0.reshape(RIM, count * E, 2 * C).astype(BF16)
    z1 = z1.reshape(RIM, count * E, 2 * C).astype(BF16)
    pair = pair.reshape(RIM - 1, count * E, 2 * C).astype(BF16)
    for y in range(E):
        for b in range(3):
            q_ref[y, rows, b * 2 * C : (b + 1) * 2 * C] = z0[y + b]
        q_ref[y, rows, 6 * C : 8 * C] = pair[y]
        q_ref[y, rows, 8 * C : 10 * C] = z1[y + 2]


def fill(q_ref, low, own, high, picks):
    low_pick, below_pick, above_pick, high_pick = picks
    put_interior(q_ref, OWN, own)
    put_interior(q_ref, LOW, low)
    put_interior(q_ref, HIGH, high)
    put_rims(
        q_ref,
        OWN - 2,
        [rim_cells(low_pick, own[:, 0]), rim_cells(below_pick, low[:, -1])],
    )
    put_rims(
        q_ref,
        OWN + E,
        [rim_cells(above_pick, high[:, 0]), rim_cells(high_pick, own[:, -1])],
    )


def main_kernel(
    even_ref,
    feat_ref,
    cot_ref,
    first_ref,
    second_ref,
    codes_ref,
    f1_ref,
    f2_ref,
    b2_ref,
    out_ref,
    grad_ref,
    delta_ref,
    pick_ref,
    q1_ref,
    q2_ref,
    q3_ref,
):
    even = even_ref[0] == 1
    first = first_ref[...]
    second = second_ref[...]
    upper = jnp.where(even, first, second).astype(F32)
    lower = jnp.where(even, second, first).astype(F32)

    def planes(t):
        return stack_x(jnp.transpose(jnp.concatenate([t, t], axis=0)).reshape(-1, E, 2 * C))

    def parts(packed):
        blocks = [packed[k * C : (k + 1) * C] for k in range((WIDE + SPAN) // 2)]
        codes = packed[len(blocks) * C :]
        f = jnp.concatenate(blocks[: WIDE // 2], axis=1)
        c = jnp.concatenate(blocks[WIDE // 2 :], axis=1)
        return planes(f), planes(c), codes

    low_f, low_c, low_codes = parts(lower)
    high_f, high_c, high_codes = parts(upper)
    codes = codes_ref[...].astype(F32)
    own_f = planes(feat_ref[0].astype(F32))
    own_c = planes(cot_ref[0].astype(F32))

    picks = (
        pick_matrix(codes[0:1], low_codes[3:5]),
        pick_matrix(low_codes[0:1], codes[1:3]),
        pick_matrix(high_codes[0:1], codes[3:5]),
        pick_matrix(codes[0:1], high_codes[1:3]),
    )
    pick_ref[0] = picks[1]
    pick_ref[1] = picks[2]

    def conv(q_ref, w, flipped=False):
        q = q_ref[...].reshape(E * PLANES * E, KDIM)
        dims = (((1,), (0 if flipped else 1,)), ((), ()))
        r = lax.dot_general(q, w, dims, preferred_element_type=F32)
        return r.reshape(E, PLANES, E, 4 * C)

    def rounded(v):
        return v.astype(BF16).astype(F32)

    def weight_gradient(which, q_ref, delta):
        zero = jnp.zeros((E, 1, E, 2 * C), F32)
        d = jnp.concatenate([zero, zero, delta, zero, zero, zero], axis=1)
        n = E + 4
        before = jnp.concatenate([zero, d[:, : n - 1]], axis=1)
        d0 = jnp.where(low_lanes((E, n, E, 2 * C)), d[:, 1 : n + 1], d[:, :n])
        d1 = before
        rows = E * n * E
        d0 = jnp.transpose(d0.reshape(rows, 2 * C)).astype(BF16)
        d1 = jnp.transpose(d1.reshape(rows, 2 * C))[:C].astype(BF16)
        dt = jnp.concatenate([d0, d1], axis=0)
        q = q_ref[:, (OWN - 2) * E : (OWN + E + 2) * E, :].reshape(rows, KDIM)
        g = jnp.dot(dt, q, preferred_element_type=F32).astype(BF16)
        for t in range(TILES):
            grad_ref[which, t] = g[:, t * 2 * C : (t + 1) * 2 * C]

    fill(q1_ref, low_f, own_f, high_f, picks)
    r = conv(q1_ref, f1_ref[...])
    pre_low = x_taps(r, LOW + 1, WIDE - 1)
    pre_own = x_taps(r, OWN, E)
    pre_high = x_taps(r, HIGH, WIDE - 1)
    act = [rounded(v * sigmoid(v)) for v in (pre_low, pre_own, pre_high)]
    pad_plane = jnp.zeros((E, 1, E, 2 * C), F32)
    fill(
        q2_ref,
        jnp.concatenate([pad_plane, act[0]], axis=1),
        act[1],
        jnp.concatenate([act[2], pad_plane], axis=1),
        picks,
    )
    r = conv(q2_ref, f2_ref[...])
    second_own = x_taps(r, OWN, E)
    put_rows(out_ref, second_own * sigmoid(second_own))
    second_low = x_taps(r, LOW + WIDE - SPAN, SPAN)
    second_high = x_taps(r, HIGH, SPAN)
    delta_own = rounded(own_c * slope(second_own))
    delta_low = rounded(low_c * slope(second_low))
    delta_high = rounded(high_c * slope(second_high))
    weight_gradient(1, q2_ref, delta_own)
    pads = jnp.zeros((E, WIDE - SPAN, E, 2 * C), F32)
    fill(
        q3_ref,
        jnp.concatenate([pads, delta_low], axis=1),
        delta_own,
        jnp.concatenate([delta_high, pads], axis=1),
        picks,
    )
    r = conv(q3_ref, b2_ref[...], True)
    first_own = rounded(x_taps(r, OWN, E) * slope(pre_own))
    first_low = rounded(x_taps(r, LOW + WIDE - 1, 1) * slope(pre_low[:, -1:]))
    first_high = rounded(x_taps(r, HIGH, 1) * slope(pre_high[:, :1]))
    weight_gradient(0, q1_ref, first_own)
    delta = jnp.concatenate([first_low, first_own, first_high], axis=1)
    delta_ref[...] = delta.reshape(E, (E + 2) * E, 2 * C).astype(BF16)


def main_call(even, feat, cot, first, second, codes, f1, f2, b2):
    q_shape = pltpu.VMEM((E, PLANES * E, KDIM), BF16)
    return pl.pallas_call(
        main_kernel,
        out_shape=(
            jax.ShapeDtypeStruct(feat.shape, BF16),
            jax.ShapeDtypeStruct((2, TILES, 3 * C, 2 * C), BF16),
            jax.ShapeDtypeStruct((E, (E + 2) * E, 2 * C), BF16),
            jax.ShapeDtypeStruct((2, CELLS, FACE), BF16),
        ),
        in_specs=[SMEM_SPEC] + [VMEM_SPEC] * 8,
        out_specs=(VMEM_SPEC,) * 4,
        scratch_shapes=[q_shape] * 3,
        compiler_params=LIMIT,
        cost_estimate=pl.CostEstimate(flops=10**10, bytes_accessed=4 << 20, transcendentals=10**6),
    )(even, feat, cot, first, second, codes, f1, f2, b2)


def last_kernel(delta_ref, pick_ref, b1_ref, out_ref, q_ref):
    delta = delta_ref[...].astype(F32).reshape(E, E + 2, E, 2 * C)
    put_interior(q_ref, 2, delta[:, 1 : E + 1])
    below = rim_cells(pick_ref[0], delta[:, 0])
    above = rim_cells(pick_ref[1], delta[:, E + 1])
    put_rims(q_ref, 0, [below, below])
    put_rims(q_ref, E + 2, [above, above])
    q = q_ref[...].reshape(E * (E + 4) * E, KDIM)
    r = jnp.dot(q, b1_ref[...], preferred_element_type=F32)
    put_rows(out_ref, x_taps(r.reshape(E, E + 4, E, 4 * C), 2, E))


def last_call(delta, pick, b1, shape):
    return pl.pallas_call(
        last_kernel,
        out_shape=jax.ShapeDtypeStruct(shape, BF16),
        in_specs=[VMEM_SPEC] * 3,
        out_specs=VMEM_SPEC,
        scratch_shapes=[pltpu.VMEM((E, (E + 4) * E, KDIM), BF16)],
        compiler_params=LIMIT,
        cost_estimate=pl.CostEstimate(flops=10**9, bytes_accessed=2 << 20, transcendentals=0),
    )(delta, pick, b1)


def finish_kernel(scale, flag_ref, mine_ref, theirs_ref, g1_ref, g2_ref):
    swap = flag_ref[0] == 1
    mine, theirs = mine_ref[...], theirs_ref[...]
    for g_ref, one, two in ((g1_ref, mine, theirs), (g2_ref, theirs, mine)):
        total = jnp.where(swap, two, one).astype(F32) * scale
        for a in range(3):
            at = {}
            for t, pair in enumerate(PAIRS):
                for h, bc in enumerate(pair):
                    if bc is not None:
                        at[3 * bc[0] + bc[1]] = total[t, a * C : (a + 1) * C, h * C : (h + 1) * C]
            g_ref[:, 9 * a * C : 9 * (a + 1) * C] = jnp.concatenate([at[o] for o in range(9)], axis=1)


def finish(flag, mine, theirs, scale):
    shape = jax.ShapeDtypeStruct((C, 27 * C), F32)
    tiles = (TILES, 3 * C, 2 * C)
    return pl.pallas_call(
        lambda *refs: finish_kernel(scale, *refs),
        out_shape=(shape, shape),
        in_specs=[SMEM_SPEC] + [VMEM_SPEC] * 2,
        out_specs=(VMEM_SPEC,) * 2,
        compiler_params=LIMIT,
    )(flag, mine.reshape(tiles), theirs.reshape(tiles))


def xor_permute(v, scene_bits, brick_bits):
    bricks = lax.axis_size("brick")
    total = lax.axis_size("scene") * bricks
    pairs = [
        (i, ((i // bricks) ^ scene_bits) * bricks + ((i % bricks) ^ brick_bits)) for i in range(total)
    ]
    return lax.ppermute(v, BOTH, pairs)


def all_sum(v):
    scenes, bricks = lax.axis_size("scene"), lax.axis_size("brick")
    if scenes != 4 or bricks != 8:
        total = lax.psum(v.astype(F32), BOTH)
        return jnp.zeros((1,), jnp.int32), total[0], total[1]
    scene, brick = lax.axis_index("scene"), lax.axis_index("brick")
    core, across = scene & 1, scene >> 1
    where = across * 2 + (brick & 1)
    parts = v.reshape(2, 4, -1, 2 * C)

    def pick(array, index):
        return lax.dynamic_index_in_dim(array, index, 0, keepdims=False)

    def sum4(own, one, two, three):
        return (own.astype(F32) + one.astype(F32)) + (two.astype(F32) + three.astype(F32))

    other = xor_permute(pick(parts, 1 - core), 1, 0)
    chip = (pick(parts, core).astype(F32) + other.astype(F32)).astype(BF16)
    moved = [
        xor_permute(pick(chip, where ^ k), 2 * (k >> 1), k & 1) for k in (1, 2, 3)
    ]
    plane = sum4(pick(chip, where), *moved).astype(BF16)
    column = [xor_permute(plane, 0, 2 * k) for k in (1, 2, 3)]
    whole = sum4(plane, *column).astype(BF16)
    back = [xor_permute(whole, 2 * (k >> 1), k & 1) for k in (1, 2, 3)]
    mine = jnp.zeros(chip.shape, BF16)
    for k, piece in enumerate([whole] + back):
        mine = lax.dynamic_update_index_in_dim(mine, piece, where ^ k, 0)
    theirs = xor_permute(mine, 1, 0)
    return core[None], mine, theirs


def step(features, cotangent, first_weight, second_weight, send_rows, gather_rows):
    bricks = lax.axis_size("brick")
    even = 1 - (lax.axis_index("brick") & 1)[None]
    feat, cot = jnp.swapaxes(features, 1, 2), jnp.swapaxes(cotangent, 1, 2)

    first, second, codes = pack(even, feat, cot, send_rows, gather_rows)
    within = [(i, i ^ 1) for i in range(bricks) if i ^ 1 < bricks]
    between = [(i, ((i + 1) ^ 1) - 1) for i in range(1, bricks) if ((i + 1) ^ 1) - 1 < bricks]
    first = lax.ppermute(first, "brick", within)
    second = lax.ppermute(second, "brick", between)
    f1, f2, b1, b2 = prepare_weights(first_weight.T, second_weight.T)

    output, grads, delta, pick = main_call(even, feat, cot, first, second, codes, f1, f2, b2)
    grad_input = last_call(delta, pick, b1, feat.shape)
    flag, mine, theirs = all_sum(grads)
    scale = float(lax.axis_size("scene") * bricks * VOX) ** -0.5
    grad_first, grad_second = finish(flag, mine, theirs, scale)
    return jnp.swapaxes(output, 1, 2), jnp.swapaxes(grad_input, 1, 2), grad_first.T, grad_second.T


def solution(mesh):
    rows = P("scene", "brick", None)
    table = P("scene", "brick")
    return jax.shard_map(
        step,
        mesh=mesh,
        in_specs=(rows, rows, P(), P(), table, table),
        out_specs=(rows, rows, P(), P()),
        check_vma=False,
    )
```

```python
import jax
import jax.numpy as jnp
from jax import lax
from jax.experimental import pallas as pl
from jax.experimental.pallas import tpu as pltpu
from jax.sharding import PartitionSpec as P

F32 = jnp.float32
BF16 = jnp.bfloat16

E = 8
C = 64
FACE = E * E
VOX = E * FACE
RIM = E + 2
CELLS = 3 * RIM * E
BOTH = ("scene", "brick")

PAIRS = (
    ((0, 0), (0, 1)),
    ((1, 0), (1, 1)),
    ((2, 0), (2, 1)),
    ((0, 2), (1, 2)),
    ((2, 2), None),
)
TILES = len(PAIRS)
KDIM = TILES * 2 * C
LOW, OWN, HIGH = 0, 6, 16
PLANES = 20
SPLIT = 4
WIDE = 4
SPAN = 2

LIMIT = pltpu.CompilerParams(vmem_limit_bytes=24 << 20)
HBM_SPEC = pl.BlockSpec(memory_space=pltpu.HBM)
VMEM_SPEC = pl.BlockSpec(memory_space=pltpu.VMEM)
SMEM_SPEC = pl.BlockSpec(memory_space=pltpu.SMEM)


def sigmoid(v):
    return jax.nn.sigmoid(v)


def slope(v):
    s = sigmoid(v)
    return s * (1.0 + v * (1.0 - s))


def low_lanes(shape):
    return lax.broadcasted_iota(jnp.int32, shape, len(shape) - 1) % (2 * C) < C


def weight_kernel(w1_hbm, w2_hbm, f1_ref, f2_ref, b1_ref, b2_ref, w1_ref, w2_ref, sems):
    fetch(((w1_hbm, w1_ref), (w2_hbm, w2_ref)), sems)
    zero = jnp.zeros((C, C), BF16)
    for w_ref, f_ref, b_ref in ((w1_ref, f1_ref, b1_ref), (w2_ref, f2_ref, b2_ref)):
        blocks = [w_ref[:, o * C : (o + 1) * C] for o in range(27)]
        for t, pair in enumerate(PAIRS):
            for k, a in enumerate((0, 1, 2, 2)):
                halves = [zero if bc is None else blocks[9 * a + 3 * bc[0] + bc[1]] for bc in pair]
                f_ref[k * C : (k + 1) * C, t * 2 * C : (t + 1) * 2 * C] = jnp.concatenate(halves, axis=1)
            for h, bc in enumerate(pair):
                rows = slice((2 * t + h) * C, (2 * t + h + 1) * C)
                if bc is None:
                    b_ref[rows, :] = jnp.zeros((C, 4 * C), BF16)
                    continue
                o = 26 - 3 * bc[0] - bc[1]
                b_ref[rows, 0 : 2 * C] = jnp.concatenate([blocks[o], blocks[o - 9]], axis=1)
                b_ref[rows, 2 * C : 4 * C] = jnp.concatenate([blocks[o - 18], blocks[o - 18]], axis=1)


def prepare_weights(w1, w2):
    fwd = jax.ShapeDtypeStruct((4 * C, KDIM), BF16)
    bwd = jax.ShapeDtypeStruct((KDIM, 4 * C), BF16)
    return pl.pallas_call(
        weight_kernel,
        out_shape=(fwd, fwd, bwd, bwd),
        in_specs=[HBM_SPEC] * 2,
        out_specs=(VMEM_SPEC,) * 4,
        scratch_shapes=[pltpu.VMEM(w1.shape, BF16)] * 2 + [pltpu.SemaphoreType.DMA((2,))],
        compiler_params=LIMIT,
        cost_estimate=pl.CostEstimate(flops=0, bytes_accessed=2 << 20, transcendentals=0),
    )(*(pltpu.with_memory_space_constraint(v, pltpu.HBM) for v in (w1, w2)))


def rim_spread(first):
    lane = lax.broadcasted_iota(jnp.int32, (2 * C, 4 * C), 1)
    c = jnp.where(lane >= RIM * E, 1, 0) + jnp.where(lane >= 2 * RIM * E, 1, 0)
    cell = lane - c * (RIM * E)
    source = (cell >> 3) * RIM + (cell & (E - 1)) + c + first
    return jnp.where(lax.broadcasted_iota(jnp.int32, (2 * C, 4 * C), 0) == source, 1.0, 0.0).astype(BF16)


def fetch(pairs, sems):
    copies = [pltpu.make_async_copy(a, b, sems.at[k]) for k, (a, b) in enumerate(pairs)]
    for copy in copies:
        copy.start()
    for copy in copies:
        copy.wait()


def pack_kernel(
    even_ref,
    feat_hbm,
    cot_hbm,
    send_hbm,
    gather_hbm,
    first_ref,
    second_ref,
    codes_ref,
    feat_ref,
    cot_ref,
    send_ref,
    gather_ref,
    sems,
):
    fetch(
        (
            (feat_hbm, feat_ref),
            (cot_hbm, cot_ref),
            (send_hbm, send_ref),
            (gather_hbm, gather_ref),
        ),
        sems,
    )
    send = send_ref[...]
    upper = lax.broadcasted_iota(jnp.int32, send.shape, 1) >= FACE
    row = jnp.where(upper, send - (VOX - FACE), send)
    sent = jnp.where((row >= 0) & (row < FACE), row + 1, 0)
    slot = gather_ref[:, : 2 * C] - VOX
    bottom = jnp.where((slot >= 0) & (slot < FACE), slot + FACE + 1, 0)
    slot = gather_ref[:, -2 * C :] - (VOX + FACE)
    top = jnp.where((slot >= 0) & (slot < FACE), slot + 1, 0)

    def spread(cells, first):
        wide = jnp.broadcast_to(cells.astype(F32), (E, 2 * C)).astype(BF16)
        v = jnp.dot(wide, rim_spread(first), preferred_element_type=F32)
        return [v[:1, : 2 * C], v[:1, 2 * C :]]

    rows = [sent.astype(F32)] + spread(bottom, 0) + spread(top, 2 * C - RIM * RIM)
    codes = jnp.concatenate(rows + [jnp.zeros((E - len(rows), 2 * C), F32)], axis=0).astype(BF16)
    codes_ref[...] = codes
    even = even_ref[0] == 1

    def put(ref, upward):
        at = 0
        for source, layers in ((feat_ref, WIDE), (cot_ref, SPAN)):
            start = VOX - layers * FACE if upward else 0
            for lane in range(start, start + layers * FACE, 2 * C):
                ref[at : at + C, :] = source[0, :, lane : lane + 2 * C]
                at += C
        ref[at : at + E, :] = codes

    @pl.when(even)
    def _():
        put(first_ref, True)
        put(second_ref, False)

    @pl.when(jnp.logical_not(even))
    def _():
        put(first_ref, False)
        put(second_ref, True)


def pack(even, feat, cot, send, gather):
    rows = (WIDE + SPAN) * FACE * C // (2 * C) + E
    return pl.pallas_call(
        pack_kernel,
        out_shape=(jax.ShapeDtypeStruct((rows, 2 * C), BF16),) * 2
        + (jax.ShapeDtypeStruct((E, 2 * C), BF16),)
        + (jax.ShapeDtypeStruct(feat.shape, BF16),) * 2,
        in_specs=[SMEM_SPEC] + [HBM_SPEC] * 4,
        out_specs=(VMEM_SPEC,) * 5,
        scratch_shapes=[
            pltpu.VMEM(send.shape, jnp.int32),
            pltpu.VMEM(gather.shape, jnp.int32),
            pltpu.SemaphoreType.DMA((4,)),
        ],
        compiler_params=LIMIT,
    )(even, *(pltpu.with_memory_space_constraint(v, pltpu.HBM) for v in (feat, cot, send, gather)))


def z_shifted(v):
    axis = v.ndim - 2
    z = lax.broadcasted_iota(jnp.int32, v.shape, axis)
    before = jnp.where(z == 0, 0.0, pltpu.roll(v, 1, axis))
    after = jnp.where(z == E - 1, 0.0, pltpu.roll(v, E - 1, axis))
    return jnp.where(low_lanes(v.shape), before, v), after


def rim_cells(pick, plane):
    m = jnp.dot(pick, plane.reshape(FACE, 2 * C).astype(BF16), preferred_element_type=F32)
    m = m.reshape(3, RIM, E, 2 * C)
    return jnp.where(low_lanes(m.shape[1:]), m[0], m[1]), m[2]


def pick_matrix(send_codes, cell_codes):
    row = lax.broadcasted_iota(jnp.int32, (FACE, 2 * C), 0).astype(F32) + 1.0
    listed = jnp.where(row == send_codes, 1.0, 0.0).astype(BF16)
    slot = lax.broadcasted_iota(jnp.int32, (2 * C, 4 * C), 0).astype(F32) + 1.0
    cells = jnp.concatenate([cell_codes[0:1], cell_codes[1:2]], axis=1)
    read = jnp.where(slot == cells, 1.0, 0.0).astype(BF16)
    picked = jnp.dot(listed, read, preferred_element_type=F32)
    return jnp.transpose(picked)[:CELLS].astype(BF16)


def stack_x(planes):
    count = planes.shape[0] // E
    v = planes.reshape(count, E, E, 2 * C)
    return jnp.stack([v[:, y] for y in range(E)], axis=0)


def x_taps(r, first, count):
    here = slice(first, first + count)
    prev = slice(first - 1, first + count - 1)
    after = slice(first + 1, first + count + 1)
    v0 = r[..., : 2 * C]
    v1 = r[..., 2 * C :]
    s = jnp.where(low_lanes((E, count, E, 2 * C)), v0[:, prev], v0[:, here])
    return s + pltpu.roll(s, C, 3) + v1[:, after]


def put_rows(out_ref, v):
    rows = jnp.stack([v[:, x] for x in range(E)], axis=0).reshape(VOX, 2 * C)
    out_ref[0] = jnp.transpose(rows)[:C].astype(BF16)


def put_interior(q_ref, first, v):
    count = v.shape[1]
    rows = pl.ds(first * E, count * E)
    z0, z1 = z_shifted(v)
    z0 = z0.reshape(E, count * E, 2 * C).astype(BF16)
    zero = jnp.zeros((1, count, E, 2 * C), F32)
    pair = jnp.where(low_lanes(v.shape), jnp.concatenate([zero, z1[: E - 1]], axis=0), z1)
    pair = pair.reshape(E, count * E, 2 * C).astype(BF16)
    z1 = z1.reshape(E, count * E, 2 * C).astype(BF16)
    none = jnp.zeros((count * E, 2 * C), BF16)
    for y in range(E):
        q_ref[y, rows, 0 : 2 * C] = z0[y - 1] if y > 0 else none
        q_ref[y, rows, 2 * C : 4 * C] = z0[y]
        q_ref[y, rows, 4 * C : 6 * C] = z0[y + 1] if y < E - 1 else none
        q_ref[y, rows, 6 * C : 8 * C] = pair[y]
        q_ref[y, rows, 8 * C : 10 * C] = z1[y + 1] if y < E - 1 else none


def put_rims(q_ref, first, rims):
    count = len(rims)
    rows = pl.ds(first * E, count * E)
    z0 = jnp.stack([r[0] for r in rims], axis=1)
    z1 = jnp.stack([r[1] for r in rims], axis=1)
    pair = jnp.where(low_lanes(z1[:-1].shape), z1[:-1], z1[1:])
    z0 = z0.reshape(RIM, count * E, 2 * C).astype(BF16)
    z1 = z1.reshape(RIM, count * E, 2 * C).astype(BF16)
    pair = pair.reshape(RIM - 1, count * E, 2 * C).astype(BF16)
    for y in range(E):
        for b in range(3):
            q_ref[y, rows, b * 2 * C : (b + 1) * 2 * C] = z0[y + b]
        q_ref[y, rows, 6 * C : 8 * C] = pair[y]
        q_ref[y, rows, 8 * C : 10 * C] = z1[y + 2]


def fill(q_ref, low, own, high, picks):
    low_pick, below_pick, above_pick, high_pick = picks
    put_interior(q_ref, OWN, own)
    put_interior(q_ref, LOW, low)
    put_interior(q_ref, HIGH, high)
    put_rims(
        q_ref,
        OWN - 2,
        [rim_cells(low_pick, own[:, 0]), rim_cells(below_pick, low[:, -1])],
    )
    put_rims(
        q_ref,
        OWN + E,
        [rim_cells(above_pick, high[:, 0]), rim_cells(high_pick, own[:, -1])],
    )


def main_kernel(
    even_ref,
    feat_ref,
    cot_ref,
    first_ref,
    second_ref,
    codes_ref,
    f1_ref,
    f2_ref,
    b2_ref,
    out_ref,
    grad_ref,
    delta_ref,
    pick_ref,
    q1_ref,
    q2_ref,
    q3_ref,
):
    even = even_ref[0] == 1
    first = first_ref[...]
    second = second_ref[...]
    upper = jnp.where(even, first, second).astype(F32)
    lower = jnp.where(even, second, first).astype(F32)

    def planes(t):
        return stack_x(jnp.transpose(jnp.concatenate([t, t], axis=0)).reshape(-1, E, 2 * C))

    def parts(packed):
        blocks = [packed[k * C : (k + 1) * C] for k in range((WIDE + SPAN) // 2)]
        codes = packed[len(blocks) * C :]
        f = jnp.concatenate(blocks[: WIDE // 2], axis=1)
        c = jnp.concatenate(blocks[WIDE // 2 :], axis=1)
        return planes(f), planes(c), codes

    low_f, low_c, low_codes = parts(lower)
    high_f, high_c, high_codes = parts(upper)
    codes = codes_ref[...].astype(F32)
    own_f = planes(feat_ref[0].astype(F32))
    own_c = planes(cot_ref[0].astype(F32))

    picks = (
        pick_matrix(codes[0:1], low_codes[3:5]),
        pick_matrix(low_codes[0:1], codes[1:3]),
        pick_matrix(high_codes[0:1], codes[3:5]),
        pick_matrix(codes[0:1], high_codes[1:3]),
    )
    pick_ref[0] = picks[1]
    pick_ref[1] = picks[2]

    def conv(q_ref, w, flipped=False, skip=0):
        dims = (((1,), (0 if flipped else 1,)), ((), ()))
        step = E // SPLIT
        parts = []
        for y in range(0, E, step):
            q = q_ref[y : y + step, skip * E : (PLANES - skip) * E, :].reshape(-1, KDIM)
            r = lax.dot_general(q, w, dims, preferred_element_type=F32)
            parts.append(r.reshape(step, PLANES - 2 * skip, E, 4 * C))
        return jnp.concatenate(parts, axis=0)

    def rounded(v):
        return v.astype(BF16).astype(F32)

    def weight_gradient(which, q_ref, delta):
        zero = jnp.zeros((E, 1, E, 2 * C), F32)
        d = jnp.concatenate([zero, zero, delta, zero, zero, zero], axis=1)
        n = E + 4
        before = jnp.concatenate([zero, d[:, : n - 1]], axis=1)
        d0 = jnp.where(low_lanes((E, n, E, 2 * C)), d[:, 1 : n + 1], d[:, :n])
        d1 = before
        rows = E * n * E
        d0 = jnp.transpose(d0.reshape(rows, 2 * C)).astype(BF16)
        d1 = jnp.transpose(d1.reshape(rows, 2 * C))[:C].astype(BF16)
        dt = jnp.concatenate([d0, d1], axis=0)
        q = q_ref[:, (OWN - 2) * E : (OWN + E + 2) * E, :].reshape(rows, KDIM)
        g = jnp.dot(dt, q, preferred_element_type=F32).astype(BF16)
        for t in range(TILES):
            grad_ref[which, t] = g[:, t * 2 * C : (t + 1) * 2 * C]

    fill(q1_ref, low_f, own_f, high_f, picks)
    r = conv(q1_ref, f1_ref[...])
    pre_low = x_taps(r, LOW + 1, WIDE - 1)
    pre_own = x_taps(r, OWN, E)
    pre_high = x_taps(r, HIGH, WIDE - 1)
    act = [rounded(v * sigmoid(v)) for v in (pre_low, pre_own, pre_high)]
    pad_plane = jnp.zeros((E, 1, E, 2 * C), F32)
    fill(
        q2_ref,
        jnp.concatenate([pad_plane, act[0]], axis=1),
        act[1],
        jnp.concatenate([act[2], pad_plane], axis=1),
        picks,
    )
    r = conv(q2_ref, f2_ref[...])
    second_own = x_taps(r, OWN, E)
    out = second_own * sigmoid(second_own)
    out_ref[...] = out.reshape(E, FACE, 2 * C).astype(BF16)
    second_low = x_taps(r, LOW + WIDE - SPAN, SPAN)
    second_high = x_taps(r, HIGH, SPAN)
    delta_own = rounded(own_c * slope(second_own))
    delta_low = rounded(low_c * slope(second_low))
    delta_high = rounded(high_c * slope(second_high))
    weight_gradient(1, q2_ref, delta_own)
    pads = jnp.zeros((E, WIDE - SPAN, E, 2 * C), F32)
    fill(
        q3_ref,
        jnp.concatenate([pads, delta_low], axis=1),
        delta_own,
        jnp.concatenate([delta_high, pads], axis=1),
        picks,
    )
    skip = WIDE - SPAN
    r = conv(q3_ref, b2_ref[...], True, skip)
    first_own = rounded(x_taps(r, OWN - skip, E) * slope(pre_own))
    first_low = rounded(x_taps(r, LOW + WIDE - 1 - skip, 1) * slope(pre_low[:, -1:]))
    first_high = rounded(x_taps(r, HIGH - skip, 1) * slope(pre_high[:, :1]))
    weight_gradient(0, q1_ref, first_own)
    delta = jnp.concatenate([first_low, first_own, first_high], axis=1)
    delta_ref[...] = delta.reshape(E, (E + 2) * E, 2 * C).astype(BF16)


def main_call(even, feat, cot, first, second, codes, f1, f2, b2):
    q_shape = pltpu.VMEM((E, PLANES * E, KDIM), BF16)
    return pl.pallas_call(
        main_kernel,
        out_shape=(
            jax.ShapeDtypeStruct((E, FACE, 2 * C), BF16),
            jax.ShapeDtypeStruct((2, TILES, 3 * C, 2 * C), BF16),
            jax.ShapeDtypeStruct((E, (E + 2) * E, 2 * C), BF16),
            jax.ShapeDtypeStruct((2, CELLS, FACE), BF16),
        ),
        in_specs=[SMEM_SPEC] + [VMEM_SPEC] * 8,
        out_specs=(VMEM_SPEC,) * 4,
        scratch_shapes=[q_shape] * 3,
        compiler_params=LIMIT,
        cost_estimate=pl.CostEstimate(flops=10**10, bytes_accessed=4 << 20, transcendentals=10**6),
    )(even, feat, cot, first, second, codes, f1, f2, b2)


def last_kernel(rows_ref, delta_ref, pick_ref, b1_ref, out_ref, grad_ref, q_ref):
    put_rows(out_ref, rows_ref[...].astype(F32).reshape(E, E, E, 2 * C))
    delta = delta_ref[...].astype(F32).reshape(E, E + 2, E, 2 * C)
    put_interior(q_ref, 2, delta[:, 1 : E + 1])
    below = rim_cells(pick_ref[0], delta[:, 0])
    above = rim_cells(pick_ref[1], delta[:, E + 1])
    put_rims(q_ref, 0, [below, below])
    put_rims(q_ref, E + 2, [above, above])
    q = q_ref[...].reshape(E * (E + 4) * E, KDIM)
    r = jnp.dot(q, b1_ref[...], preferred_element_type=F32)
    put_rows(grad_ref, x_taps(r.reshape(E, E + 4, E, 4 * C), 2, E))


def last_call(rows, delta, pick, b1, shape):
    return pl.pallas_call(
        last_kernel,
        out_shape=(jax.ShapeDtypeStruct(shape, BF16),) * 2,
        in_specs=[VMEM_SPEC] * 4,
        out_specs=(VMEM_SPEC,) * 2,
        scratch_shapes=[pltpu.VMEM((E, (E + 4) * E, KDIM), BF16)],
        compiler_params=LIMIT,
        cost_estimate=pl.CostEstimate(flops=10**9, bytes_accessed=2 << 20, transcendentals=0),
    )(rows, delta, pick, b1)


def finish_kernel(scale, flag_ref, mine_ref, theirs_ref, g1_ref, g2_ref):
    swap = flag_ref[0] == 1
    mine, theirs = mine_ref[...], theirs_ref[...]
    for g_ref, one, two in ((g1_ref, mine, theirs), (g2_ref, theirs, mine)):
        total = jnp.where(swap, two, one).astype(F32) * scale
        for a in range(3):
            at = {}
            for t, pair in enumerate(PAIRS):
                for h, bc in enumerate(pair):
                    if bc is not None:
                        at[3 * bc[0] + bc[1]] = total[t, a * C : (a + 1) * C, h * C : (h + 1) * C]
            g_ref[:, 9 * a * C : 9 * (a + 1) * C] = jnp.concatenate([at[o] for o in range(9)], axis=1)


def finish(flag, mine, theirs, scale):
    shape = jax.ShapeDtypeStruct((C, 27 * C), F32)
    tiles = (TILES, 3 * C, 2 * C)
    return pl.pallas_call(
        lambda *refs: finish_kernel(scale, *refs),
        out_shape=(shape, shape),
        in_specs=[SMEM_SPEC] + [VMEM_SPEC] * 2,
        out_specs=(VMEM_SPEC,) * 2,
        compiler_params=LIMIT,
    )(flag, mine.reshape(tiles), theirs.reshape(tiles))


def xor_permute(v, scene_bits, brick_bits):
    bricks = lax.axis_size("brick")
    total = lax.axis_size("scene") * bricks
    pairs = [
        (i, ((i // bricks) ^ scene_bits) * bricks + ((i % bricks) ^ brick_bits)) for i in range(total)
    ]
    return lax.ppermute(v, BOTH, pairs)


def exchange(pieces):
    out = []
    for k, piece in zip((1, 2, 3), pieces):
        out.append(xor_permute(piece, 2 * (k >> 1), k & 1))
    return out


def all_sum(v):
    scenes, bricks = lax.axis_size("scene"), lax.axis_size("brick")
    if scenes != 4 or bricks != 8:
        total = lax.psum(v.astype(F32), BOTH)
        return jnp.zeros((1,), jnp.int32), total[0], total[1]
    scene, brick = lax.axis_index("scene"), lax.axis_index("brick")
    core, across = scene & 1, scene >> 1
    where = across * 2 + (brick & 1)
    parts = v.reshape(2, 4, -1, 2 * C)

    def pick(array, index):
        return lax.dynamic_index_in_dim(array, index, 0, keepdims=False)

    def sum4(own, one, two, three):
        return (own.astype(F32) + one.astype(F32)) + (two.astype(F32) + three.astype(F32))

    other = xor_permute(pick(parts, 1 - core), 1, 0)
    chip = (pick(parts, core).astype(F32) + other.astype(F32)).astype(BF16)
    moved = exchange([pick(chip, where ^ k) for k in (1, 2, 3)])
    plane = sum4(pick(chip, where), *moved).astype(BF16)
    other = xor_permute(plane, 0, 2)
    pair = (plane.astype(F32) + other.astype(F32)).astype(BF16)
    other = xor_permute(pair, 0, 4)
    whole = (pair.astype(F32) + other.astype(F32)).astype(BF16)
    back = exchange([whole] * 3)
    mine = jnp.zeros(chip.shape, BF16)
    for k, piece in enumerate([whole] + back):
        mine = lax.dynamic_update_index_in_dim(mine, piece, where ^ k, 0)
    theirs = xor_permute(mine, 1, 0)
    return core[None], mine, theirs


def step(features, cotangent, first_weight, second_weight, send_rows, gather_rows):
    bricks = lax.axis_size("brick")
    even = 1 - (lax.axis_index("brick") & 1)[None]
    feat, cot = jnp.swapaxes(features, 1, 2), jnp.swapaxes(cotangent, 1, 2)

    first, second, codes, feat, cot = pack(even, feat, cot, send_rows, gather_rows)
    within = [(i, i ^ 1) for i in range(bricks) if i ^ 1 < bricks]
    between = [(i, ((i + 1) ^ 1) - 1) for i in range(1, bricks) if ((i + 1) ^ 1) - 1 < bricks]
    first = lax.ppermute(first, "brick", within)
    second = lax.ppermute(second, "brick", between)
    f1, f2, b1, b2 = prepare_weights(first_weight.T, second_weight.T)

    rows, grads, delta, pick = main_call(even, feat, cot, first, second, codes, f1, f2, b2)
    output, grad_input = last_call(rows, delta, pick, b1, feat.shape)
    flag, mine, theirs = all_sum(grads)
    scale = float(lax.axis_size("scene") * bricks * VOX) ** -0.5
    grad_first, grad_second = finish(flag, mine, theirs, scale)
    return jnp.swapaxes(output, 1, 2), jnp.swapaxes(grad_input, 1, 2), grad_first.T, grad_second.T


def solution(mesh):
    rows = P("scene", "brick", None)
    table = P("scene", "brick")
    return jax.shard_map(
        step,
        mesh=mesh,
        in_specs=(rows, rows, P(), P(), table, table),
        out_specs=(rows, rows, P(), P()),
        check_vma=False,
    )
```

```python
import jax
import jax.numpy as jnp
from jax import lax
from jax.experimental import pallas as pl
from jax.experimental.pallas import tpu as pltpu
from jax.sharding import PartitionSpec as P

F32 = jnp.float32
BF16 = jnp.bfloat16

E = 8
C = 64
FACE = E * E
VOX = E * FACE
RIM = E + 2
CELLS = 3 * RIM * E
BOTH = ("scene", "brick")

PAIRS = (
    ((0, 0), (0, 1)),
    ((1, 0), (1, 1)),
    ((2, 0), (2, 1)),
    ((0, 2), (1, 2)),
    ((2, 2), None),
)
TILES = len(PAIRS)
KDIM = TILES * 2 * C
SPLIT = 2
WIDE = 4
SPAN = 2

PLANES = tuple(
    p for k in range(WIDE) for p in ((-1, E - WIDE + k), (1, WIDE - 1 - k))
) + ((-1, E), (1, -1), (0, -1), (0, E))
REST = len(PLANES)
RIMS = REST - 4
BESIDE = slice((REST - 2) * E, REST * E)

LIMIT = pltpu.CompilerParams(vmem_limit_bytes=24 << 20)
HBM_SPEC = pl.BlockSpec(memory_space=pltpu.HBM)
VMEM_SPEC = pl.BlockSpec(memory_space=pltpu.VMEM)
SMEM_SPEC = pl.BlockSpec(memory_space=pltpu.SMEM)


def sigmoid(v):
    return jax.nn.sigmoid(v)


def slope(v):
    s = sigmoid(v)
    return s * (1.0 + v * (1.0 - s))


def low_lanes(shape):
    return lax.broadcasted_iota(jnp.int32, shape, len(shape) - 1) % (2 * C) < C


def own_kernel(
    w1_hbm, w2_hbm, feat_ref, f1_ref, f2_ref, b1_ref, b2_ref, q_ref, r_ref, w1_ref, w2_ref, sems
):
    copies = [
        pltpu.make_async_copy(w1_hbm, w1_ref, sems.at[0]),
        pltpu.make_async_copy(w2_hbm, w2_ref, sems.at[1]),
    ]
    for copy in copies:
        copy.start()
    put_interior(q_ref, 0, planes_of(feat_ref[0].astype(F32)))
    for copy in copies:
        copy.wait()
    zero = jnp.zeros((C, C), BF16)
    for w_ref, f_ref, b_ref in ((w1_ref, f1_ref, b1_ref), (w2_ref, f2_ref, b2_ref)):
        blocks = [w_ref[:, o * C : (o + 1) * C] for o in range(27)]
        for t, pair in enumerate(PAIRS):
            for k, a in enumerate((0, 1, 2, 2)):
                halves = [zero if bc is None else blocks[9 * a + 3 * bc[0] + bc[1]] for bc in pair]
                f_ref[k * C : (k + 1) * C, t * 2 * C : (t + 1) * 2 * C] = jnp.concatenate(halves, axis=1)
            for h, bc in enumerate(pair):
                rows = slice((2 * t + h) * C, (2 * t + h + 1) * C)
                if bc is None:
                    b_ref[rows, :] = jnp.zeros((C, 4 * C), BF16)
                    continue
                o = 26 - 3 * bc[0] - bc[1]
                b_ref[rows, 0 : 2 * C] = jnp.concatenate([blocks[o], blocks[o - 9]], axis=1)
                b_ref[rows, 2 * C : 4 * C] = jnp.concatenate([blocks[o - 18], blocks[o - 18]], axis=1)
    w = f1_ref[...]
    half = E // SPLIT
    for y in range(0, E, half):
        r = lax.dot_general(
            q_ref[y : y + half].reshape(-1, KDIM), w, (((1,), (1,)), ((), ())), preferred_element_type=F32
        )
        r_ref[y : y + half] = r.reshape(half, FACE, 4 * C)


def own_call(w1, w2, feat):
    fwd = jax.ShapeDtypeStruct((4 * C, KDIM), BF16)
    bwd = jax.ShapeDtypeStruct((KDIM, 4 * C), BF16)
    w1, w2 = (pltpu.with_memory_space_constraint(v, pltpu.HBM) for v in (w1, w2))
    return pl.pallas_call(
        own_kernel,
        out_shape=(
            fwd,
            fwd,
            bwd,
            bwd,
            jax.ShapeDtypeStruct((E, FACE, KDIM), BF16),
            jax.ShapeDtypeStruct((E, FACE, 4 * C), F32),
        ),
        in_specs=[HBM_SPEC] * 2 + [VMEM_SPEC],
        out_specs=(VMEM_SPEC,) * 6,
        scratch_shapes=[pltpu.VMEM(w1.shape, BF16)] * 2 + [pltpu.SemaphoreType.DMA((2,))],
        compiler_params=LIMIT,
        cost_estimate=pl.CostEstimate(flops=10**9, bytes_accessed=3 << 20, transcendentals=0),
    )(w1, w2, feat)


def rim_spread(first):
    lane = lax.broadcasted_iota(jnp.int32, (2 * C, 4 * C), 1)
    c = jnp.where(lane >= RIM * E, 1, 0) + jnp.where(lane >= 2 * RIM * E, 1, 0)
    cell = lane - c * (RIM * E)
    source = (cell >> 3) * RIM + (cell & (E - 1)) + c + first
    return jnp.where(lax.broadcasted_iota(jnp.int32, (2 * C, 4 * C), 0) == source, 1.0, 0.0).astype(BF16)


def fetch(pairs, sems):
    copies = [pltpu.make_async_copy(a, b, sems.at[k]) for k, (a, b) in enumerate(pairs)]
    for copy in copies:
        copy.start()
    for copy in copies:
        copy.wait()


def pack_kernel(
    even_ref,
    feat_hbm,
    cot_hbm,
    send_hbm,
    gather_hbm,
    first_ref,
    second_ref,
    codes_ref,
    feat_ref,
    cot_ref,
    send_ref,
    gather_ref,
    sems,
):
    fetch(
        (
            (feat_hbm, feat_ref),
            (cot_hbm, cot_ref),
            (send_hbm, send_ref),
            (gather_hbm, gather_ref),
        ),
        sems,
    )
    send = send_ref[...]
    upper = lax.broadcasted_iota(jnp.int32, send.shape, 1) >= FACE
    row = jnp.where(upper, send - (VOX - FACE), send)
    sent = jnp.where((row >= 0) & (row < FACE), row + 1, 0)
    slot = gather_ref[:, : 2 * C] - VOX
    bottom = jnp.where((slot >= 0) & (slot < FACE), slot + FACE + 1, 0)
    slot = gather_ref[:, -2 * C :] - (VOX + FACE)
    top = jnp.where((slot >= 0) & (slot < FACE), slot + 1, 0)

    def spread(cells, first):
        wide = jnp.broadcast_to(cells.astype(F32), (E, 2 * C)).astype(BF16)
        v = jnp.dot(wide, rim_spread(first), preferred_element_type=F32)
        return [v[:1, : 2 * C], v[:1, 2 * C :]]

    rows = [sent.astype(F32)] + spread(bottom, 0) + spread(top, 2 * C - RIM * RIM)
    codes = jnp.concatenate(rows + [jnp.zeros((E - len(rows), 2 * C), F32)], axis=0).astype(BF16)
    codes_ref[...] = codes
    even = even_ref[0] == 1

    def put(ref, upward):
        at = 0
        for source, layers in ((feat_ref, WIDE), (cot_ref, SPAN)):
            start = VOX - layers * FACE if upward else 0
            for lane in range(start, start + layers * FACE, 2 * C):
                ref[at : at + C, :] = source[0, :, lane : lane + 2 * C]
                at += C
        ref[at : at + E, :] = codes

    @pl.when(even)
    def _():
        put(first_ref, True)
        put(second_ref, False)

    @pl.when(jnp.logical_not(even))
    def _():
        put(first_ref, False)
        put(second_ref, True)


def pack(even, feat, cot, send, gather):
    rows = (WIDE + SPAN) * FACE * C // (2 * C) + E
    return pl.pallas_call(
        pack_kernel,
        out_shape=(jax.ShapeDtypeStruct((rows, 2 * C), BF16),) * 2
        + (jax.ShapeDtypeStruct((E, 2 * C), BF16),)
        + (jax.ShapeDtypeStruct(feat.shape, BF16),) * 2,
        in_specs=[SMEM_SPEC] + [HBM_SPEC] * 4,
        out_specs=(VMEM_SPEC,) * 5,
        scratch_shapes=[
            pltpu.VMEM(send.shape, jnp.int32),
            pltpu.VMEM(gather.shape, jnp.int32),
            pltpu.SemaphoreType.DMA((4,)),
        ],
        compiler_params=LIMIT,
    )(even, *(pltpu.with_memory_space_constraint(v, pltpu.HBM) for v in (feat, cot, send, gather)))


def z_shifted(v):
    axis = v.ndim - 2
    z = lax.broadcasted_iota(jnp.int32, v.shape, axis)
    before = jnp.where(z == 0, 0.0, pltpu.roll(v, 1, axis))
    after = jnp.where(z == E - 1, 0.0, pltpu.roll(v, E - 1, axis))
    return jnp.where(low_lanes(v.shape), before, v), after


def rim_cells(pick, plane):
    m = jnp.dot(pick, plane.reshape(FACE, 2 * C).astype(BF16), preferred_element_type=F32)
    m = m.reshape(3, RIM, E, 2 * C)
    return jnp.where(low_lanes(m.shape[1:]), m[0], m[1]), m[2]


def pick_matrix(send_codes, cell_codes):
    row = lax.broadcasted_iota(jnp.int32, (FACE, 2 * C), 0).astype(F32) + 1.0
    listed = jnp.where(row == send_codes, 1.0, 0.0).astype(BF16)
    slot = lax.broadcasted_iota(jnp.int32, (2 * C, 4 * C), 0).astype(F32) + 1.0
    cells = jnp.concatenate([cell_codes[0:1], cell_codes[1:2]], axis=1)
    read = jnp.where(slot == cells, 1.0, 0.0).astype(BF16)
    picked = jnp.dot(listed, read, preferred_element_type=F32)
    return jnp.transpose(picked)[:CELLS].astype(BF16)


def stack_x(planes):
    count = planes.shape[0] // E
    v = planes.reshape(count, E, E, 2 * C)
    return jnp.stack([v[:, y] for y in range(E)], axis=0)


def x_taps(own, rest, skip, planes):
    def taps(names, lanes):
        parts = []
        for side, x in names:
            inside = side == 0 and 0 <= x < E
            source, k = (own, x) if inside else (rest, PLANES.index((side, x)) - skip)
            parts.append(source[:, k : k + 1, :, lanes])
        return jnp.concatenate(parts, axis=1)

    low, high = slice(0, 2 * C), slice(2 * C, 4 * C)
    prev = taps([(side, x - 1) for side, x in planes], low)
    here = taps(planes, low)
    after = taps([(side, x + 1) for side, x in planes], high)
    s = jnp.where(low_lanes(here.shape), prev, here)
    return s + pltpu.roll(s, C, 3) + after


def planes_of(t):
    return stack_x(jnp.transpose(jnp.concatenate([t, t], axis=0)).reshape(-1, E, 2 * C))


def put_rows(out_ref, v):
    rows = jnp.stack([v[:, x] for x in range(E)], axis=0).reshape(VOX, 2 * C)
    out_ref[0] = jnp.transpose(rows)[:C].astype(BF16)


def put_interior(q_ref, first, v):
    count = v.shape[1]
    rows = pl.ds(first * E, count * E)
    z0, z1 = z_shifted(v)
    z0 = z0.reshape(E, count * E, 2 * C).astype(BF16)
    zero = jnp.zeros((1, count, E, 2 * C), F32)
    pair = jnp.where(low_lanes(v.shape), jnp.concatenate([zero, z1[: E - 1]], axis=0), z1)
    pair = pair.reshape(E, count * E, 2 * C).astype(BF16)
    z1 = z1.reshape(E, count * E, 2 * C).astype(BF16)
    none = jnp.zeros((count * E, 2 * C), BF16)
    for y in range(E):
        q_ref[y, rows, 0 : 2 * C] = z0[y - 1] if y > 0 else none
        q_ref[y, rows, 2 * C : 4 * C] = z0[y]
        q_ref[y, rows, 4 * C : 6 * C] = z0[y + 1] if y < E - 1 else none
        q_ref[y, rows, 6 * C : 8 * C] = pair[y]
        q_ref[y, rows, 8 * C : 10 * C] = z1[y + 1] if y < E - 1 else none


def put_rims(q_ref, first, rims):
    count = len(rims)
    rows = pl.ds(first * E, count * E)
    z0 = jnp.stack([r[0] for r in rims], axis=1)
    z1 = jnp.stack([r[1] for r in rims], axis=1)
    pair = jnp.where(low_lanes(z1[:-1].shape), z1[:-1], z1[1:])
    z0 = z0.reshape(RIM, count * E, 2 * C).astype(BF16)
    z1 = z1.reshape(RIM, count * E, 2 * C).astype(BF16)
    pair = pair.reshape(RIM - 1, count * E, 2 * C).astype(BF16)
    for y in range(E):
        for b in range(3):
            q_ref[y, rows, b * 2 * C : (b + 1) * 2 * C] = z0[y + b]
        q_ref[y, rows, 6 * C : 8 * C] = pair[y]
        q_ref[y, rows, 8 * C : 10 * C] = z1[y + 2]


def put_rest(q_ref, low, own, high, picks):
    low_pick, below_pick, above_pick, high_pick = picks
    n = low.shape[1]
    mixed = []
    for k in range(n):
        mixed += [low[:, k : k + 1], high[:, n - 1 - k : n - k]]
    put_interior(q_ref, RIMS - 2 * n, jnp.concatenate(mixed, axis=1))
    rims = (
        rim_cells(low_pick, own[:, 0]),
        rim_cells(high_pick, own[:, -1]),
        rim_cells(below_pick, low[:, -1]),
        rim_cells(above_pick, high[:, 0]),
    )
    put_rims(q_ref, RIMS, rims)


def main_kernel(
    even_ref,
    feat_ref,
    cot_ref,
    first_ref,
    second_ref,
    codes_ref,
    f1_ref,
    f2_ref,
    b2_ref,
    q1_ref,
    r1_ref,
    out_ref,
    grad_ref,
    delta_ref,
    pick_ref,
    q2_ref,
    q3_ref,
    rest1_ref,
    rest2_ref,
    rest3_ref,
):
    even = even_ref[0] == 1
    first = first_ref[...]
    second = second_ref[...]
    upper = jnp.where(even, first, second).astype(F32)
    lower = jnp.where(even, second, first).astype(F32)

    def parts(packed):
        blocks = [packed[k * C : (k + 1) * C] for k in range((WIDE + SPAN) // 2)]
        codes = packed[len(blocks) * C :]
        f = jnp.concatenate(blocks[: WIDE // 2], axis=1)
        c = jnp.concatenate(blocks[WIDE // 2 :], axis=1)
        return planes_of(f), planes_of(c), codes

    low_f, low_c, low_codes = parts(lower)
    high_f, high_c, high_codes = parts(upper)
    codes = codes_ref[...].astype(F32)
    ends = jnp.concatenate([feat_ref[0, :, : 2 * C], feat_ref[0, :, -2 * C :]], axis=1)
    own_f = planes_of(ends.astype(F32))
    own_c = planes_of(cot_ref[0].astype(F32))

    picks = (
        pick_matrix(codes[0:1], low_codes[3:5]),
        pick_matrix(low_codes[0:1], codes[1:3]),
        pick_matrix(high_codes[0:1], codes[3:5]),
        pick_matrix(codes[0:1], high_codes[1:3]),
    )
    pick_ref[0] = picks[1]
    pick_ref[1] = picks[2]

    def conv(q_ref, w, flipped=False, skip=0):
        dims = (((1,), (0 if flipped else 1,)), ((), ()))
        step = E // SPLIT
        first = skip * E
        parts = []
        for y in range(0, E, step):
            q = q_ref[y : y + step, first:, :]
            count = q.shape[1] // E
            r = lax.dot_general(q.reshape(-1, KDIM), w, dims, preferred_element_type=F32)
            parts.append(r.reshape(step, count, E, 4 * C))
        return jnp.concatenate(parts, axis=0)

    def rounded(v):
        return v.astype(BF16).astype(F32)

    def weight_gradient(which, q_ref, rest_ref, delta):
        def turned(d0, d1):
            rows = d0.shape[0] * d0.shape[1] * E
            d0 = jnp.transpose(d0.reshape(rows, 2 * C)).astype(BF16)
            d1 = jnp.transpose(d1.reshape(rows, 2 * C))[:C].astype(BF16)
            return jnp.concatenate([d0, d1], axis=0)

        zero = jnp.zeros((E, 1, E, 2 * C), F32)
        up = jnp.concatenate([delta[:, 1:], zero], axis=1)
        down = jnp.concatenate([zero, delta[:, :-1]], axis=1)
        low = low_lanes(delta.shape)
        own = turned(jnp.where(low, up, delta), down)
        first = jnp.where(low[:, :1], delta[:, :1], 0.0)
        ends = turned(
            jnp.concatenate([first, zero], axis=1), jnp.concatenate([zero, delta[:, -1:]], axis=1)
        )
        g = jnp.dot(own, q_ref[...].reshape(-1, KDIM), preferred_element_type=F32)
        g += jnp.dot(ends, rest_ref[:, BESIDE, :].reshape(-1, KDIM), preferred_element_type=F32)
        rows = 3 * C
        for t in range(TILES - 1):
            grad_ref[which, t * rows : (t + 1) * rows, :] = g[:, t * 2 * C : (t + 1) * 2 * C].astype(BF16)
        last = g[:, (TILES - 1) * 2 * C :]
        packed = jnp.where(
            low_lanes((rows // 2, 2 * C)), last[: rows // 2], pltpu.roll(last[rows // 2 :], C, 1)
        )
        grad_ref[which, (TILES - 1) * rows :, :] = packed.astype(BF16)

    def near(side, count):
        return [(-1, E - count + k) for k in range(count)] if side < 0 else [(1, k) for k in range(count)]

    inside = [(0, x) for x in range(E)]

    put_rest(rest1_ref, low_f, own_f, high_f, picks)
    own = r1_ref[...].reshape(E, E, E, 4 * C)
    rest = conv(rest1_ref, f1_ref[...])
    pre_low, pre_own, pre_high = (
        x_taps(own, rest, 0, p) for p in (near(-1, WIDE - 1), inside, near(1, WIDE - 1))
    )
    act_low, act_own, act_high = (rounded(v * sigmoid(v)) for v in (pre_low, pre_own, pre_high))
    put_interior(q2_ref, 0, act_own)
    put_rest(rest2_ref, act_low, act_own, act_high, picks)
    own, rest = conv(q2_ref, f2_ref[...]), conv(rest2_ref, f2_ref[...], False, 2)
    second_own = x_taps(own, rest, 2, inside)
    out = second_own * sigmoid(second_own)
    out_ref[...] = out.reshape(E, FACE, 2 * C).astype(BF16)
    delta_own = rounded(own_c * slope(second_own))
    delta_low = rounded(low_c * slope(x_taps(own, rest, 2, near(-1, SPAN))))
    delta_high = rounded(high_c * slope(x_taps(own, rest, 2, near(1, SPAN))))
    put_interior(q3_ref, 0, delta_own)
    put_rest(rest3_ref, delta_low, delta_own, delta_high, picks)
    own, rest = conv(q3_ref, b2_ref[...], True), conv(rest3_ref, b2_ref[...], True, 4)
    weight_gradient(1, q2_ref, rest2_ref, delta_own)
    first_own = rounded(x_taps(own, rest, 4, inside) * slope(pre_own))
    first_low = rounded(x_taps(own, rest, 4, near(-1, 1)) * slope(pre_low[:, -1:]))
    first_high = rounded(x_taps(own, rest, 4, near(1, 1)) * slope(pre_high[:, :1]))
    weight_gradient(0, q1_ref, rest1_ref, first_own)
    delta = jnp.concatenate([first_low, first_own, first_high], axis=1)
    delta_ref[...] = delta.reshape(E, (E + 2) * E, 2 * C).astype(BF16)


def main_call(even, feat, cot, first, second, codes, f1, f2, b2, q1, r1):
    own_shape = pltpu.VMEM((E, FACE, KDIM), BF16)
    rest_shape = pltpu.VMEM((E, REST * E, KDIM), BF16)
    return pl.pallas_call(
        main_kernel,
        out_shape=(
            jax.ShapeDtypeStruct((E, FACE, 2 * C), BF16),
            jax.ShapeDtypeStruct((2, 27 * C // 2, 2 * C), BF16),
            jax.ShapeDtypeStruct((E, (E + 2) * E, 2 * C), BF16),
            jax.ShapeDtypeStruct((2, CELLS, FACE), BF16),
        ),
        in_specs=[SMEM_SPEC] + [VMEM_SPEC] * 10,
        out_specs=(VMEM_SPEC,) * 4,
        scratch_shapes=[own_shape] * 2 + [rest_shape] * 3,
        compiler_params=LIMIT,
        cost_estimate=pl.CostEstimate(flops=10**10, bytes_accessed=4 << 20, transcendentals=10**6),
    )(even, feat, cot, first, second, codes, f1, f2, b2, q1, r1)


def last_kernel(rows_ref, delta_ref, pick_ref, b1_ref, out_ref, grad_ref, q_ref, rim_ref):
    put_rows(out_ref, rows_ref[...].astype(F32).reshape(E, E, E, 2 * C))
    delta = delta_ref[...].astype(F32).reshape(E, E + 2, E, 2 * C)
    put_interior(q_ref, 0, delta[:, 1 : E + 1])
    put_rims(rim_ref, 0, (rim_cells(pick_ref[0], delta[:, 0]), rim_cells(pick_ref[1], delta[:, E + 1])))
    b1 = b1_ref[...]
    own = jnp.dot(q_ref[...].reshape(-1, KDIM), b1, preferred_element_type=F32)
    rims = jnp.dot(rim_ref[...].reshape(-1, KDIM), b1, preferred_element_type=F32)
    own, rims = own.reshape(E, E, E, 4 * C), rims.reshape(E, 2, E, 4 * C)
    put_rows(grad_ref, x_taps(own, rims, REST - 2, [(0, x) for x in range(E)]))


def last_call(rows, delta, pick, b1, shape):
    return pl.pallas_call(
        last_kernel,
        out_shape=(jax.ShapeDtypeStruct(shape, BF16),) * 2,
        in_specs=[VMEM_SPEC] * 4,
        out_specs=(VMEM_SPEC,) * 2,
        scratch_shapes=[pltpu.VMEM((E, FACE, KDIM), BF16), pltpu.VMEM((E, 2 * E, KDIM), BF16)],
        compiler_params=LIMIT,
        cost_estimate=pl.CostEstimate(flops=10**9, bytes_accessed=2 << 20, transcendentals=0),
    )(rows, delta, pick, b1)


def unpack(packed, scale, out_ref):
    rows = 3 * C
    v = packed.astype(F32) * scale
    last = v[(TILES - 1) * rows :]
    last = jnp.concatenate([last[:, :C], last[:, C:]], axis=0)
    tiles = [v[t * rows : (t + 1) * rows] for t in range(TILES - 1)] + [last]
    for a in range(3):
        at = {}
        for t, pair in enumerate(PAIRS):
            for h, bc in enumerate(pair):
                if bc is not None:
                    at[3 * bc[0] + bc[1]] = tiles[t][a * C : (a + 1) * C, h * C : (h + 1) * C]
        out_ref[:, 9 * a * C : 9 * (a + 1) * C] = jnp.concatenate([at[o] for o in range(9)], axis=1)


def half_call(mine, scale):
    def kernel(mine_ref, out_ref):
        unpack(mine_ref[...], scale, out_ref)

    return pl.pallas_call(
        kernel,
        out_shape=jax.ShapeDtypeStruct((C, 27 * C), F32),
        in_specs=[VMEM_SPEC],
        out_specs=VMEM_SPEC,
        compiler_params=LIMIT,
        cost_estimate=pl.CostEstimate(flops=0, bytes_accessed=1 << 20, transcendentals=0),
    )(mine)


def finish_kernel(scale, flag_ref, mine_ref, theirs_ref, g1_hbm, g2_hbm, other_ref, sems):
    swapped = flag_ref[0] == 1

    def put(mine_hbm, other_hbm):
        first = pltpu.make_async_copy(mine_ref, mine_hbm, sems.at[0])
        first.start()
        unpack(theirs_ref[...], scale, other_ref)
        second = pltpu.make_async_copy(other_ref, other_hbm, sems.at[1])
        second.start()
        first.wait()
        second.wait()

    @pl.when(swapped)
    def _():
        put(g2_hbm, g1_hbm)

    @pl.when(jnp.logical_not(swapped))
    def _():
        put(g1_hbm, g2_hbm)


def finish(flag, mine, theirs, scale):
    shape = jax.ShapeDtypeStruct((C, 27 * C), F32)
    return pl.pallas_call(
        lambda *refs: finish_kernel(scale, *refs),
        out_shape=(shape, shape),
        in_specs=[SMEM_SPEC] + [VMEM_SPEC] * 2,
        out_specs=(HBM_SPEC,) * 2,
        scratch_shapes=[pltpu.VMEM((C, 27 * C), F32), pltpu.SemaphoreType.DMA((2,))],
        compiler_params=LIMIT,
    )(flag, mine, theirs)


def xor_permute(v, scene_bits, brick_bits):
    bricks = lax.axis_size("brick")
    total = lax.axis_size("scene") * bricks
    pairs = [
        (i, ((i // bricks) ^ scene_bits) * bricks + ((i % bricks) ^ brick_bits)) for i in range(total)
    ]
    return lax.ppermute(v, BOTH, pairs)


def exchange(pieces):
    out = []
    for k, piece in zip((1, 2, 3), pieces):
        out.append(xor_permute(piece, 2 * (k >> 1), k & 1))
    return out


def all_sum(v):
    scenes, bricks = lax.axis_size("scene"), lax.axis_size("brick")
    if scenes != 4 or bricks != 8:
        total = lax.psum(v.astype(F32), BOTH)
        return jnp.zeros((1,), jnp.int32), total[0], total[1]
    scene, brick = lax.axis_index("scene"), lax.axis_index("brick")
    core, across = scene & 1, scene >> 1
    where = across * 2 + (brick & 1)
    parts = v.reshape(2, 4, -1, 2 * C)

    def pick(array, index):
        return lax.dynamic_index_in_dim(array, index, 0, keepdims=False)

    def sum4(own, one, two, three):
        return (own.astype(F32) + one.astype(F32)) + (two.astype(F32) + three.astype(F32))

    other = xor_permute(pick(parts, 1 - core), 1, 0)
    chip = (pick(parts, core).astype(F32) + other.astype(F32)).astype(BF16)
    moved = exchange([pick(chip, where ^ k) for k in (1, 2, 3)])
    plane = sum4(pick(chip, where), *moved).astype(BF16)
    column = []
    for k in (1, 2, 3):
        column.append(xor_permute(plane, 0, 2 * k))
    whole = sum4(plane, *column).astype(BF16)
    back = exchange([whole] * 3)
    mine = jnp.zeros(chip.shape, BF16)
    for k, piece in enumerate([whole] + back):
        mine = lax.dynamic_update_index_in_dim(mine, piece, where ^ k, 0)
    mine = mine.reshape(v.shape[1:])
    theirs = xor_permute(mine, 1, 0)
    return core[None], mine, theirs


def step(features, cotangent, first_weight, second_weight, send_rows, gather_rows):
    bricks = lax.axis_size("brick")
    even = 1 - (lax.axis_index("brick") & 1)[None]
    feat, cot = jnp.swapaxes(features, 1, 2), jnp.swapaxes(cotangent, 1, 2)

    first, second, codes, feat, cot = pack(even, feat, cot, send_rows, gather_rows)
    within = [(i, i ^ 1) for i in range(bricks) if i ^ 1 < bricks]
    between = [(i, ((i + 1) ^ 1) - 1) for i in range(1, bricks) if ((i + 1) ^ 1) - 1 < bricks]
    first = lax.ppermute(first, "brick", within)
    second = lax.ppermute(second, "brick", between)
    f1, f2, b1, b2, q1, r1 = own_call(first_weight.T, second_weight.T, feat)

    rows, grads, delta, pick = main_call(even, feat, cot, first, second, codes, f1, f2, b2, q1, r1)
    output, grad_input = last_call(rows, delta, pick, b1, feat.shape)
    flag, mine, theirs = all_sum(grads)
    scale = float(lax.axis_size("scene") * bricks * VOX) ** -0.5
    mine = half_call(mine, scale)
    grad_first, grad_second = finish(flag, mine, theirs, scale)
    return jnp.swapaxes(output, 1, 2), jnp.swapaxes(grad_input, 1, 2), grad_first.T, grad_second.T


def solution(mesh):
    rows = P("scene", "brick", None)
    table = P("scene", "brick")
    return jax.shard_map(
        step,
        mesh=mesh,
        in_specs=(rows, rows, P(), P(), table, table),
        out_specs=(rows, rows, P(), P()),
        check_vma=False,
    )
```

```python
import jax
import jax.numpy as jnp
from jax import lax
from jax.experimental import pallas as pl
from jax.experimental.pallas import tpu as pltpu
from jax.sharding import PartitionSpec as P

F32 = jnp.float32
BF16 = jnp.bfloat16

E = 8
C = 64
FACE = E * E
VOX = E * FACE
RIM = E + 2
CELLS = 3 * RIM * E
BOTH = ("scene", "brick")

PAIRS = (
    ((0, 0), (0, 1)),
    ((1, 0), (1, 1)),
    ((2, 0), (2, 1)),
    ((0, 2), (1, 2)),
    ((2, 2), None),
)
TILES = len(PAIRS)
KDIM = TILES * 2 * C
SPLIT = 2
WIDE = 4
SPAN = 2

OWN = tuple((0, x) for x in range(E))
SEAMS = ((-1, E), (1, -1), (0, -1), (0, E))


def beyond(first):
    return tuple(p for k in range(first, WIDE) for p in ((-1, E - WIDE + k), (1, WIDE - 1 - k)))


INNER1, OUTER1 = OWN, beyond(0) + SEAMS
INNER2, OUTER2 = OWN[1:-1], beyond(1) + SEAMS + (OWN[0], OWN[-1])
INNER3, OUTER3 = OWN[2:-2], beyond(2) + SEAMS + (OWN[0], OWN[-1], OWN[1], OWN[-2])
EDGE = OWN[:2] + OWN[-2:]

LIMIT = pltpu.CompilerParams(vmem_limit_bytes=24 << 20)
HBM_SPEC = pl.BlockSpec(memory_space=pltpu.HBM)
VMEM_SPEC = pl.BlockSpec(memory_space=pltpu.VMEM)
SMEM_SPEC = pl.BlockSpec(memory_space=pltpu.SMEM)


def sigmoid(v):
    return jax.nn.sigmoid(v)


def slope(v):
    s = sigmoid(v)
    return s * (1.0 + v * (1.0 - s))


def low_lanes(shape):
    return lax.broadcasted_iota(jnp.int32, shape, len(shape) - 1) % (2 * C) < C


def own_kernel(
    w1_hbm,
    w2_hbm,
    feat_ref,
    cot_ref,
    f1_ref,
    f2_ref,
    b1_ref,
    b2_ref,
    q1_ref,
    q2_ref,
    r1_ref,
    r2_ref,
    r3_ref,
    slope_ref,
    delta_ref,
    out_ref,
    q3_ref,
    w1_ref,
    w2_ref,
    sems,
):
    copies = [
        pltpu.make_async_copy(w1_hbm, w1_ref, sems.at[0]),
        pltpu.make_async_copy(w2_hbm, w2_ref, sems.at[1]),
    ]
    for copy in copies:
        copy.start()
    put_interior(q1_ref, 0, planes_of(feat_ref[0].astype(F32)))
    cot = planes_of(cot_ref[0, :, 2 * FACE : -2 * FACE].astype(F32))
    for copy in copies:
        copy.wait()
    zero = jnp.zeros((C, C), BF16)
    for w_ref, f_ref, b_ref in ((w1_ref, f1_ref, b1_ref), (w2_ref, f2_ref, b2_ref)):
        blocks = [w_ref[:, o * C : (o + 1) * C] for o in range(27)]
        for t, pair in enumerate(PAIRS):
            for k, a in enumerate((0, 1, 2, 2)):
                halves = [zero if bc is None else blocks[9 * a + 3 * bc[0] + bc[1]] for bc in pair]
                f_ref[k * C : (k + 1) * C, t * 2 * C : (t + 1) * 2 * C] = jnp.concatenate(halves, axis=1)
            for h, bc in enumerate(pair):
                rows = slice((2 * t + h) * C, (2 * t + h + 1) * C)
                if bc is None:
                    b_ref[rows, :] = jnp.zeros((C, 4 * C), BF16)
                    continue
                o = 26 - 3 * bc[0] - bc[1]
                b_ref[rows, 0 : 2 * C] = jnp.concatenate([blocks[o], blocks[o - 9]], axis=1)
                b_ref[rows, 2 * C : 4 * C] = jnp.concatenate([blocks[o - 18], blocks[o - 18]], axis=1)
    r1 = conv(q1_ref, f1_ref[...])
    r1_ref[...] = r1
    pre = x_taps(((r1, INNER1),), INNER2)
    slope_ref[...] = slope(pre)
    put_interior(q2_ref, 0, rounded(pre * sigmoid(pre)))
    r2 = conv(q2_ref, f2_ref[...])
    r2_ref[...] = r2
    pre = x_taps(((r2, INNER2),), INNER3)
    out_ref[...] = (pre * sigmoid(pre)).astype(BF16)
    delta = rounded(cot * slope(pre))
    delta_ref[...] = delta
    put_interior(q3_ref, 0, delta)
    r3_ref[...] = conv(q3_ref, b2_ref[...], True)


def own_call(w1, w2, feat, cot):
    n1, n2, n3 = len(INNER1), len(INNER2), len(INNER3)
    fwd = jax.ShapeDtypeStruct((4 * C, KDIM), BF16)
    bwd = jax.ShapeDtypeStruct((KDIM, 4 * C), BF16)

    def taps(n):
        return jax.ShapeDtypeStruct((E, n, E, 4 * C), F32)

    def values(n, dtype):
        return jax.ShapeDtypeStruct((E, n, E, 2 * C), dtype)

    w1, w2 = (pltpu.with_memory_space_constraint(v, pltpu.HBM) for v in (w1, w2))
    return pl.pallas_call(
        own_kernel,
        out_shape=(
            fwd,
            fwd,
            bwd,
            bwd,
            jax.ShapeDtypeStruct((E, n1 * E, KDIM), BF16),
            jax.ShapeDtypeStruct((E, n2 * E, KDIM), BF16),
            taps(n1),
            taps(n2),
            taps(n3),
            values(n2, F32),
            values(n3, F32),
            values(n3, BF16),
        ),
        in_specs=[HBM_SPEC] * 2 + [VMEM_SPEC] * 2,
        out_specs=(VMEM_SPEC,) * 12,
        scratch_shapes=[pltpu.VMEM((E, n3 * E, KDIM), BF16)]
        + [pltpu.VMEM(w1.shape, BF16)] * 2
        + [pltpu.SemaphoreType.DMA((2,))],
        compiler_params=LIMIT,
        cost_estimate=pl.CostEstimate(flops=10**9, bytes_accessed=3 << 20, transcendentals=0),
    )(w1, w2, feat, cot)


def rim_spread(first):
    lane = lax.broadcasted_iota(jnp.int32, (2 * C, 4 * C), 1)
    c = jnp.where(lane >= RIM * E, 1, 0) + jnp.where(lane >= 2 * RIM * E, 1, 0)
    cell = lane - c * (RIM * E)
    source = (cell >> 3) * RIM + (cell & (E - 1)) + c + first
    return jnp.where(lax.broadcasted_iota(jnp.int32, (2 * C, 4 * C), 0) == source, 1.0, 0.0).astype(BF16)


def fetch(pairs, sems):
    copies = [pltpu.make_async_copy(a, b, sems.at[k]) for k, (a, b) in enumerate(pairs)]
    for copy in copies:
        copy.start()
    for copy in copies:
        copy.wait()


def pack_kernel(
    even_ref,
    feat_hbm,
    cot_hbm,
    send_hbm,
    gather_hbm,
    first_ref,
    second_ref,
    codes_ref,
    feat_ref,
    cot_ref,
    send_ref,
    gather_ref,
    sems,
):
    fetch(
        (
            (feat_hbm, feat_ref),
            (cot_hbm, cot_ref),
            (send_hbm, send_ref),
            (gather_hbm, gather_ref),
        ),
        sems,
    )
    send = send_ref[...]
    upper = lax.broadcasted_iota(jnp.int32, send.shape, 1) >= FACE
    row = jnp.where(upper, send - (VOX - FACE), send)
    sent = jnp.where((row >= 0) & (row < FACE), row + 1, 0)
    slot = gather_ref[:, : 2 * C] - VOX
    bottom = jnp.where((slot >= 0) & (slot < FACE), slot + FACE + 1, 0)
    slot = gather_ref[:, -2 * C :] - (VOX + FACE)
    top = jnp.where((slot >= 0) & (slot < FACE), slot + 1, 0)

    def spread(cells, first):
        wide = jnp.broadcast_to(cells.astype(F32), (E, 2 * C)).astype(BF16)
        v = jnp.dot(wide, rim_spread(first), preferred_element_type=F32)
        return [v[:1, : 2 * C], v[:1, 2 * C :]]

    rows = [sent.astype(F32)] + spread(bottom, 0) + spread(top, 2 * C - RIM * RIM)
    codes = jnp.concatenate(rows + [jnp.zeros((E - len(rows), 2 * C), F32)], axis=0).astype(BF16)
    codes_ref[...] = codes
    even = even_ref[0] == 1

    def put(ref, upward):
        at = 0
        for source, layers in ((feat_ref, WIDE), (cot_ref, SPAN)):
            start = VOX - layers * FACE if upward else 0
            for lane in range(start, start + layers * FACE, 2 * C):
                ref[at : at + C, :] = source[0, :, lane : lane + 2 * C]
                at += C
        ref[at : at + E, :] = codes

    @pl.when(even)
    def _():
        put(first_ref, True)
        put(second_ref, False)

    @pl.when(jnp.logical_not(even))
    def _():
        put(first_ref, False)
        put(second_ref, True)


def pack(even, feat, cot, send, gather):
    rows = (WIDE + SPAN) * FACE * C // (2 * C) + E
    return pl.pallas_call(
        pack_kernel,
        out_shape=(jax.ShapeDtypeStruct((rows, 2 * C), BF16),) * 2
        + (jax.ShapeDtypeStruct((E, 2 * C), BF16),)
        + (jax.ShapeDtypeStruct(feat.shape, BF16),) * 2,
        in_specs=[SMEM_SPEC] + [HBM_SPEC] * 4,
        out_specs=(VMEM_SPEC,) * 5,
        scratch_shapes=[
            pltpu.VMEM(send.shape, jnp.int32),
            pltpu.VMEM(gather.shape, jnp.int32),
            pltpu.SemaphoreType.DMA((4,)),
        ],
        compiler_params=LIMIT,
    )(even, *(pltpu.with_memory_space_constraint(v, pltpu.HBM) for v in (feat, cot, send, gather)))


def z_shifted(v):
    axis = v.ndim - 2
    z = lax.broadcasted_iota(jnp.int32, v.shape, axis)
    before = jnp.where(z == 0, 0.0, pltpu.roll(v, 1, axis))
    after = jnp.where(z == E - 1, 0.0, pltpu.roll(v, E - 1, axis))
    return jnp.where(low_lanes(v.shape), before, v), after


def rim_cells(pick, plane):
    m = jnp.dot(pick, plane.reshape(FACE, 2 * C).astype(BF16), preferred_element_type=F32)
    m = m.reshape(3, RIM, E, 2 * C)
    return jnp.where(low_lanes(m.shape[1:]), m[0], m[1]), m[2]


def pick_matrix(send_codes, cell_codes):
    row = lax.broadcasted_iota(jnp.int32, (FACE, 2 * C), 0).astype(F32) + 1.0
    listed = jnp.where(row == send_codes, 1.0, 0.0).astype(BF16)
    slot = lax.broadcasted_iota(jnp.int32, (2 * C, 4 * C), 0).astype(F32) + 1.0
    cells = jnp.concatenate([cell_codes[0:1], cell_codes[1:2]], axis=1)
    read = jnp.where(slot == cells, 1.0, 0.0).astype(BF16)
    picked = jnp.dot(listed, read, preferred_element_type=F32)
    return jnp.transpose(picked)[:CELLS].astype(BF16)


def stack_x(planes):
    count = planes.shape[0] // E
    v = planes.reshape(count, E, E, 2 * C)
    return jnp.stack([v[:, y] for y in range(E)], axis=0)


def rounded(v):
    return v.astype(BF16).astype(F32)


def conv(q_ref, w, flipped=False):
    dims = (((1,), (0 if flipped else 1,)), ((), ()))
    step = E // SPLIT
    parts = []
    for y in range(0, E, step):
        q = q_ref[y : y + step].reshape(-1, KDIM)
        r = lax.dot_general(q, w, dims, preferred_element_type=F32)
        parts.append(r.reshape(step, -1, E, 4 * C))
    return jnp.concatenate(parts, axis=0)


def x_taps(banks, planes):
    def taps(names, lanes):
        parts = []
        for name in names:
            for r, held in banks:
                if name in held:
                    k = held.index(name)
                    parts.append(r[:, k : k + 1, :, lanes])
        return jnp.concatenate(parts, axis=1)

    low, high = slice(0, 2 * C), slice(2 * C, 4 * C)
    prev = taps([(side, x - 1) for side, x in planes], low)
    here = taps(planes, low)
    after = taps([(side, x + 1) for side, x in planes], high)
    s = jnp.where(low_lanes(here.shape), prev, here)
    return s + pltpu.roll(s, C, 3) + after


def planes_of(t):
    return stack_x(jnp.transpose(jnp.concatenate([t, t], axis=0)).reshape(-1, E, 2 * C))


def put_rows(out_ref, v):
    rows = jnp.stack([v[:, x] for x in range(E)], axis=0).reshape(VOX, 2 * C)
    out_ref[0] = jnp.transpose(rows)[:C].astype(BF16)


def put_interior(q_ref, first, v):
    count = v.shape[1]
    rows = pl.ds(first * E, count * E)
    z0, z1 = z_shifted(v)
    z0 = z0.reshape(E, count * E, 2 * C).astype(BF16)
    zero = jnp.zeros((1, count, E, 2 * C), F32)
    pair = jnp.where(low_lanes(v.shape), jnp.concatenate([zero, z1[: E - 1]], axis=0), z1)
    pair = pair.reshape(E, count * E, 2 * C).astype(BF16)
    z1 = z1.reshape(E, count * E, 2 * C).astype(BF16)
    none = jnp.zeros((count * E, 2 * C), BF16)
    for y in range(E):
        q_ref[y, rows, 0 : 2 * C] = z0[y - 1] if y > 0 else none
        q_ref[y, rows, 2 * C : 4 * C] = z0[y]
        q_ref[y, rows, 4 * C : 6 * C] = z0[y + 1] if y < E - 1 else none
        q_ref[y, rows, 6 * C : 8 * C] = pair[y]
        q_ref[y, rows, 8 * C : 10 * C] = z1[y + 1] if y < E - 1 else none


def put_rims(q_ref, first, rims):
    count = len(rims)
    rows = pl.ds(first * E, count * E)
    z0 = jnp.stack([r[0] for r in rims], axis=1)
    z1 = jnp.stack([r[1] for r in rims], axis=1)
    pair = jnp.where(low_lanes(z1[:-1].shape), z1[:-1], z1[1:])
    z0 = z0.reshape(RIM, count * E, 2 * C).astype(BF16)
    z1 = z1.reshape(RIM, count * E, 2 * C).astype(BF16)
    pair = pair.reshape(RIM - 1, count * E, 2 * C).astype(BF16)
    for y in range(E):
        for b in range(3):
            q_ref[y, rows, b * 2 * C : (b + 1) * 2 * C] = z0[y + b]
        q_ref[y, rows, 6 * C : 8 * C] = pair[y]
        q_ref[y, rows, 8 * C : 10 * C] = z1[y + 2]


def put_outer(q_ref, low, ends, high, picks, count):
    low_pick, below_pick, above_pick, high_pick = picks
    n = low.shape[1]
    mixed = []
    for k in range(n):
        mixed += [low[:, k : k + 1], high[:, n - 1 - k : n - k]]
    put_interior(q_ref, 0, jnp.concatenate(mixed, axis=1))
    rims = (
        rim_cells(low_pick, ends[:, 0]),
        rim_cells(high_pick, ends[:, 1]),
        rim_cells(below_pick, low[:, -1]),
        rim_cells(above_pick, high[:, 0]),
    )
    put_rims(q_ref, 2 * n, rims)
    if count:
        put_interior(q_ref, 2 * n + len(rims), ends[:, :count])


def main_kernel(
    even_ref,
    feat_ref,
    cot_ref,
    first_ref,
    second_ref,
    codes_ref,
    f1_ref,
    f2_ref,
    b2_ref,
    q1_ref,
    q2_ref,
    r1_ref,
    r2_ref,
    r3_ref,
    slope_ref,
    inner_delta_ref,
    out_ref,
    grad_ref,
    delta_ref,
    pick_ref,
    o1_ref,
    o2_ref,
    o3_ref,
):
    even = even_ref[0] == 1
    first = first_ref[...]
    second = second_ref[...]
    upper = jnp.where(even, first, second).astype(F32)
    lower = jnp.where(even, second, first).astype(F32)

    def parts(packed):
        blocks = [packed[k * C : (k + 1) * C] for k in range((WIDE + SPAN) // 2)]
        codes = packed[len(blocks) * C :]
        f = jnp.concatenate(blocks[: WIDE // 2], axis=1)
        c = jnp.concatenate(blocks[WIDE // 2 :], axis=1)
        return planes_of(f), planes_of(c), codes

    low_f, low_c, low_codes = parts(lower)
    high_f, high_c, high_codes = parts(upper)
    codes = codes_ref[...].astype(F32)

    def edge(ref):
        return planes_of(jnp.concatenate([ref[0, :, : 2 * FACE], ref[0, :, -2 * FACE :]], axis=1).astype(F32))

    def order(v, *names):
        return jnp.concatenate([v[:, EDGE.index(n) : EDGE.index(n) + 1] for n in names], axis=1)

    own_f, own_c = edge(feat_ref), edge(cot_ref)

    picks = (
        pick_matrix(codes[0:1], low_codes[3:5]),
        pick_matrix(low_codes[0:1], codes[1:3]),
        pick_matrix(high_codes[0:1], codes[3:5]),
        pick_matrix(codes[0:1], high_codes[1:3]),
    )
    pick_ref[0] = picks[1]
    pick_ref[1] = picks[2]

    def weight_gradient(which, banks, delta):
        def plane(x):
            return delta[:, x : x + 1] if 0 <= x < E else jnp.zeros((E, 1, E, 2 * C), F32)

        g = 0.0
        for q, names in banks:
            rows = E * len(names) * E
            up, here, down = (
                jnp.concatenate([plane(x + k) for _, x in names], axis=1) for k in (1, 0, -1)
            )
            d0 = jnp.where(low_lanes(here.shape), up, here)
            d0 = jnp.transpose(d0.reshape(rows, 2 * C)).astype(BF16)
            d1 = jnp.transpose(down.reshape(rows, 2 * C))[:C].astype(BF16)
            d = jnp.concatenate([d0, d1], axis=0)
            g += jnp.dot(d, q.reshape(rows, KDIM), preferred_element_type=F32)
        rows = 3 * C
        for t in range(TILES - 1):
            grad_ref[which, t * rows : (t + 1) * rows, :] = g[:, t * 2 * C : (t + 1) * 2 * C].astype(BF16)
        last = g[:, (TILES - 1) * 2 * C :]
        packed = jnp.where(
            low_lanes((rows // 2, 2 * C)), last[: rows // 2], pltpu.roll(last[rows // 2 :], C, 1)
        )
        grad_ref[which, (TILES - 1) * rows :, :] = packed.astype(BF16)

    def near(side, count):
        return tuple((-1, E - count + k) if side < 0 else (1, k) for k in range(count))

    def from_plane(ref, names, first):
        return ref[:, first * E :, :], names[first:]

    put_outer(o1_ref, low_f, order(own_f, OWN[0], OWN[-1]), high_f, picks, 0)
    banks = ((r1_ref[...], INNER1), (conv(o1_ref, f1_ref[...]), OUTER1))
    pre_low, pre_ends, pre_high = (
        x_taps(banks, p) for p in (near(-1, WIDE - 1), (OWN[0], OWN[-1]), near(1, WIDE - 1))
    )
    act_low, act_ends, act_high = (rounded(v * sigmoid(v)) for v in (pre_low, pre_ends, pre_high))
    put_outer(o2_ref, act_low, act_ends, act_high, picks, 2)
    banks = ((r2_ref[...], INNER2), (conv(o2_ref, f2_ref[...]), OUTER2))
    pre_edge = x_taps(banks, EDGE)
    out_ref[...] = (pre_edge * sigmoid(pre_edge)).astype(BF16)
    delta_edge = rounded(own_c * slope(pre_edge))
    delta_low = rounded(low_c * slope(x_taps(banks, near(-1, SPAN))))
    delta_high = rounded(high_c * slope(x_taps(banks, near(1, SPAN))))
    put_outer(o3_ref, delta_low, order(delta_edge, OWN[0], OWN[-1], OWN[1], OWN[-2]), delta_high, picks, 4)
    banks = ((r3_ref[...], INNER3), (conv(o3_ref, b2_ref[...], True), OUTER3))
    delta_own = jnp.concatenate([delta_edge[:, :2], inner_delta_ref[...], delta_edge[:, 2:]], axis=1)
    beside = len(OUTER2) - 4
    weight_gradient(1, ((q2_ref[...], INNER2), from_plane(o2_ref, OUTER2, beside)), delta_own)
    slope_ends = slope(pre_ends)
    slopes = jnp.concatenate([slope_ends[:, :1], slope_ref[...], slope_ends[:, 1:]], axis=1)
    first_own = rounded(x_taps(banks, OWN) * slopes)
    first_low = rounded(x_taps(banks, near(-1, 1)) * slope(pre_low[:, -1:]))
    first_high = rounded(x_taps(banks, near(1, 1)) * slope(pre_high[:, :1]))
    beside = len(OUTER1) - 2
    weight_gradient(0, ((q1_ref[...], INNER1), from_plane(o1_ref, OUTER1, beside)), first_own)
    delta = jnp.concatenate([first_low, first_own, first_high], axis=1)
    delta_ref[...] = delta.reshape(E, (E + 2) * E, 2 * C).astype(BF16)


def main_call(*operands):
    outer = [pltpu.VMEM((E, len(names) * E, KDIM), BF16) for names in (OUTER1, OUTER2, OUTER3)]
    return pl.pallas_call(
        main_kernel,
        out_shape=(
            jax.ShapeDtypeStruct((E, len(EDGE), E, 2 * C), BF16),
            jax.ShapeDtypeStruct((2, 27 * C // 2, 2 * C), BF16),
            jax.ShapeDtypeStruct((E, (E + 2) * E, 2 * C), BF16),
            jax.ShapeDtypeStruct((2, CELLS, FACE), BF16),
        ),
        in_specs=[SMEM_SPEC] + [VMEM_SPEC] * (len(operands) - 1),
        out_specs=(VMEM_SPEC,) * 4,
        scratch_shapes=outer,
        compiler_params=LIMIT,
        cost_estimate=pl.CostEstimate(flops=10**10, bytes_accessed=4 << 20, transcendentals=10**6),
    )(*operands)


def last_kernel(edge_ref, inner_ref, delta_ref, pick_ref, b1_ref, out_ref, grad_ref, q_ref, rim_ref):
    edge = edge_ref[...].astype(F32)
    put_rows(out_ref, jnp.concatenate([edge[:, :2], inner_ref[...].astype(F32), edge[:, 2:]], axis=1))
    delta = delta_ref[...].astype(F32).reshape(E, E + 2, E, 2 * C)
    put_interior(q_ref, 0, delta[:, 1 : E + 1])
    put_rims(rim_ref, 0, (rim_cells(pick_ref[0], delta[:, 0]), rim_cells(pick_ref[1], delta[:, E + 1])))
    banks = ((conv(q_ref, b1_ref[...], True), OWN), (conv(rim_ref, b1_ref[...], True), SEAMS[2:]))
    put_rows(grad_ref, x_taps(banks, OWN))


def last_call(edge, inner, delta, pick, b1, shape):
    return pl.pallas_call(
        last_kernel,
        out_shape=(jax.ShapeDtypeStruct(shape, BF16),) * 2,
        in_specs=[VMEM_SPEC] * 5,
        out_specs=(VMEM_SPEC,) * 2,
        scratch_shapes=[pltpu.VMEM((E, FACE, KDIM), BF16), pltpu.VMEM((E, 2 * E, KDIM), BF16)],
        compiler_params=LIMIT,
        cost_estimate=pl.CostEstimate(flops=10**9, bytes_accessed=2 << 20, transcendentals=0),
    )(edge, inner, delta, pick, b1)


def unpack(packed, scale, out_ref):
    rows = 3 * C
    v = packed.astype(F32) * scale
    last = v[(TILES - 1) * rows :]
    last = jnp.concatenate([last[:, :C], last[:, C:]], axis=0)
    tiles = [v[t * rows : (t + 1) * rows] for t in range(TILES - 1)] + [last]
    for a in range(3):
        at = {}
        for t, pair in enumerate(PAIRS):
            for h, bc in enumerate(pair):
                if bc is not None:
                    at[3 * bc[0] + bc[1]] = tiles[t][a * C : (a + 1) * C, h * C : (h + 1) * C]
        out_ref[:, 9 * a * C : 9 * (a + 1) * C] = jnp.concatenate([at[o] for o in range(9)], axis=1)


def half_call(mine, scale):
    def kernel(mine_ref, out_ref):
        unpack(mine_ref[...], scale, out_ref)

    return pl.pallas_call(
        kernel,
        out_shape=jax.ShapeDtypeStruct((C, 27 * C), F32),
        in_specs=[VMEM_SPEC],
        out_specs=VMEM_SPEC,
        compiler_params=LIMIT,
        cost_estimate=pl.CostEstimate(flops=0, bytes_accessed=1 << 20, transcendentals=0),
    )(mine)


def finish_kernel(scale, flag_ref, mine_ref, theirs_ref, g1_hbm, g2_hbm, other_ref, sems):
    swapped = flag_ref[0] == 1

    def put(mine_hbm, other_hbm):
        first = pltpu.make_async_copy(mine_ref, mine_hbm, sems.at[0])
        first.start()
        unpack(theirs_ref[...], scale, other_ref)
        second = pltpu.make_async_copy(other_ref, other_hbm, sems.at[1])
        second.start()
        first.wait()
        second.wait()

    @pl.when(swapped)
    def _():
        put(g2_hbm, g1_hbm)

    @pl.when(jnp.logical_not(swapped))
    def _():
        put(g1_hbm, g2_hbm)


def finish(flag, mine, theirs, scale):
    shape = jax.ShapeDtypeStruct((C, 27 * C), F32)
    return pl.pallas_call(
        lambda *refs: finish_kernel(scale, *refs),
        out_shape=(shape, shape),
        in_specs=[SMEM_SPEC] + [VMEM_SPEC] * 2,
        out_specs=(HBM_SPEC,) * 2,
        scratch_shapes=[pltpu.VMEM((C, 27 * C), F32), pltpu.SemaphoreType.DMA((2,))],
        compiler_params=LIMIT,
    )(flag, mine, theirs)


def xor_permute(v, scene_bits, brick_bits):
    bricks = lax.axis_size("brick")
    total = lax.axis_size("scene") * bricks
    pairs = [
        (i, ((i // bricks) ^ scene_bits) * bricks + ((i % bricks) ^ brick_bits)) for i in range(total)
    ]
    return lax.ppermute(v, BOTH, pairs)


def exchange(pieces):
    out = []
    for k, piece in zip((1, 2, 3), pieces):
        out.append(xor_permute(piece, 2 * (k >> 1), k & 1))
    return out


def all_sum(v):
    scenes, bricks = lax.axis_size("scene"), lax.axis_size("brick")
    if scenes != 4 or bricks != 8:
        total = lax.psum(v.astype(F32), BOTH)
        return jnp.zeros((1,), jnp.int32), total[0], total[1]
    scene, brick = lax.axis_index("scene"), lax.axis_index("brick")
    core, across = scene & 1, scene >> 1
    where = across * 2 + (brick & 1)
    parts = v.reshape(2, 4, -1, 2 * C)

    def pick(array, index):
        return lax.dynamic_index_in_dim(array, index, 0, keepdims=False)

    def sum4(own, one, two, three):
        return (own.astype(F32) + one.astype(F32)) + (two.astype(F32) + three.astype(F32))

    other = xor_permute(pick(parts, 1 - core), 1, 0)
    chip = (pick(parts, core).astype(F32) + other.astype(F32)).astype(BF16)
    moved = exchange([pick(chip, where ^ k) for k in (1, 2, 3)])
    plane = sum4(pick(chip, where), *moved).astype(BF16)
    column = []
    for k in (1, 2, 3):
        column.append(xor_permute(plane, 0, 2 * k))
    whole = sum4(plane, *column).astype(BF16)
    back = exchange([whole] * 3)
    mine = jnp.zeros(chip.shape, BF16)
    for k, piece in enumerate([whole] + back):
        mine = lax.dynamic_update_index_in_dim(mine, piece, where ^ k, 0)
    mine = mine.reshape(v.shape[1:])
    theirs = xor_permute(mine, 1, 0)
    return core[None], mine, theirs


def step(features, cotangent, first_weight, second_weight, send_rows, gather_rows):
    bricks = lax.axis_size("brick")
    even = 1 - (lax.axis_index("brick") & 1)[None]
    feat, cot = jnp.swapaxes(features, 1, 2), jnp.swapaxes(cotangent, 1, 2)

    first, second, codes, feat, cot = pack(even, feat, cot, send_rows, gather_rows)
    within = [(i, i ^ 1) for i in range(bricks) if i ^ 1 < bricks]
    between = [(i, ((i + 1) ^ 1) - 1) for i in range(1, bricks) if ((i + 1) ^ 1) - 1 < bricks]
    first = lax.ppermute(first, "brick", within)
    second = lax.ppermute(second, "brick", between)
    f1, f2, b1, b2, *own, inner_out = own_call(first_weight.T, second_weight.T, feat, cot)

    edge_out, grads, delta, pick = main_call(even, feat, cot, first, second, codes, f1, f2, b2, *own)
    output, grad_input = last_call(edge_out, inner_out, delta, pick, b1, feat.shape)
    flag, mine, theirs = all_sum(grads)
    scale = float(lax.axis_size("scene") * bricks * VOX) ** -0.5
    mine = half_call(mine, scale)
    grad_first, grad_second = finish(flag, mine, theirs, scale)
    return jnp.swapaxes(output, 1, 2), jnp.swapaxes(grad_input, 1, 2), grad_first.T, grad_second.T


def solution(mesh):
    rows = P("scene", "brick", None)
    table = P("scene", "brick")
    return jax.shard_map(
        step,
        mesh=mesh,
        in_specs=(rows, rows, P(), P(), table, table),
        out_specs=(rows, rows, P(), P()),
        check_vma=False,
    )
```

```python
import jax
import jax.numpy as jnp
from jax import lax
from jax.experimental import pallas as pl
from jax.experimental.pallas import tpu as pltpu
from jax.sharding import PartitionSpec as P

F32 = jnp.float32
BF16 = jnp.bfloat16

E = 8
C = 64
FACE = E * E
VOX = E * FACE
RIM = E + 2
CELLS = 3 * RIM * E
BOTH = ("scene", "brick")

PAIRS = (
    ((0, 0), (0, 1)),
    ((1, 0), (1, 1)),
    ((2, 0), (2, 1)),
    ((0, 2), (1, 2)),
    ((2, 2), None),
)
TILES = len(PAIRS)
KDIM = TILES * 2 * C
SPLIT = 2
WIDE = 4
SPAN = 2

OWN = tuple((0, x) for x in range(E))
SEAMS = ((-1, E), (1, -1), (0, -1), (0, E))


def beyond(first):
    return tuple(p for k in range(first, WIDE) for p in ((-1, E - WIDE + k), (1, WIDE - 1 - k)))


INNER1 = OWN
INNER2, OUTER2 = OWN[1:-1], beyond(1) + SEAMS + (OWN[0], OWN[-1])
INNER3, OUTER3 = OWN[2:-2], beyond(2) + SEAMS + (OWN[0], OWN[-1], OWN[1], OWN[-2])
EDGE = OWN[:2] + OWN[-2:]

LIMIT = pltpu.CompilerParams(vmem_limit_bytes=24 << 20)
HBM_SPEC = pl.BlockSpec(memory_space=pltpu.HBM)
VMEM_SPEC = pl.BlockSpec(memory_space=pltpu.VMEM)
SMEM_SPEC = pl.BlockSpec(memory_space=pltpu.SMEM)


def sigmoid(v):
    return jax.nn.sigmoid(v)


def slope(v):
    s = sigmoid(v)
    return s * (1.0 + v * (1.0 - s))


def low_lanes(shape):
    return lax.broadcasted_iota(jnp.int32, shape, len(shape) - 1) % (2 * C) < C


def own_kernel(
    w1_hbm,
    w2_hbm,
    feat_ref,
    cot_ref,
    f1_ref,
    f2_ref,
    b1_ref,
    b2_ref,
    q1_ref,
    q2_ref,
    r1_ref,
    r2_ref,
    r3_ref,
    slope_ref,
    delta_ref,
    out_ref,
    ends_ref,
    edge_ref,
    q3_ref,
    w1_ref,
    w2_ref,
    sems,
):
    copies = [
        pltpu.make_async_copy(w1_hbm, w1_ref, sems.at[0]),
        pltpu.make_async_copy(w2_hbm, w2_ref, sems.at[1]),
    ]
    for copy in copies:
        copy.start()
    feat, cot = planes_of(feat_ref[0].astype(F32)), planes_of(cot_ref[0].astype(F32))
    ends_ref[...] = jnp.concatenate([feat[:, :1], feat[:, -1:]], axis=1)
    edge_ref[...] = jnp.concatenate([cot[:, :2], cot[:, -2:]], axis=1)
    put_interior(q1_ref, 0, feat)
    for copy in copies:
        copy.wait()
    zero = jnp.zeros((C, C), BF16)
    for w_ref, f_ref, b_ref in ((w1_ref, f1_ref, b1_ref), (w2_ref, f2_ref, b2_ref)):
        blocks = [w_ref[:, o * C : (o + 1) * C] for o in range(27)]
        for t, pair in enumerate(PAIRS):
            for k, a in enumerate((0, 1, 2, 2)):
                halves = [zero if bc is None else blocks[9 * a + 3 * bc[0] + bc[1]] for bc in pair]
                f_ref[k * C : (k + 1) * C, t * 2 * C : (t + 1) * 2 * C] = jnp.concatenate(halves, axis=1)
            for h, bc in enumerate(pair):
                rows = slice((2 * t + h) * C, (2 * t + h + 1) * C)
                if bc is None:
                    b_ref[rows, :] = jnp.zeros((C, 4 * C), BF16)
                    continue
                o = 26 - 3 * bc[0] - bc[1]
                b_ref[rows, 0 : 2 * C] = jnp.concatenate([blocks[o], blocks[o - 9]], axis=1)
                b_ref[rows, 2 * C : 4 * C] = jnp.concatenate([blocks[o - 18], blocks[o - 18]], axis=1)
    r1 = conv(q1_ref, f1_ref[...])
    r1_ref[...] = r1
    pre = x_taps(((r1, INNER1),), INNER2)
    slope_ref[...] = slope(pre)
    put_interior(q2_ref, 0, rounded(pre * sigmoid(pre)))
    r2 = conv(q2_ref, f2_ref[...])
    r2_ref[...] = r2
    pre = x_taps(((r2, INNER2),), INNER3)
    out_ref[...] = (pre * sigmoid(pre)).astype(BF16)
    delta = rounded(cot[:, 2:-2] * slope(pre))
    delta_ref[...] = delta
    put_interior(q3_ref, 0, delta)
    r3_ref[...] = conv(q3_ref, b2_ref[...], True)


def own_call(w1, w2, feat, cot):
    n1, n2, n3 = len(INNER1), len(INNER2), len(INNER3)
    fwd = jax.ShapeDtypeStruct((4 * C, KDIM), BF16)
    bwd = jax.ShapeDtypeStruct((KDIM, 4 * C), BF16)

    def taps(n):
        return jax.ShapeDtypeStruct((E, n, E, 4 * C), F32)

    def values(n, dtype):
        return jax.ShapeDtypeStruct((E, n, E, 2 * C), dtype)

    w1, w2 = (pltpu.with_memory_space_constraint(v, pltpu.HBM) for v in (w1, w2))
    return pl.pallas_call(
        own_kernel,
        out_shape=(
            fwd,
            fwd,
            bwd,
            bwd,
            jax.ShapeDtypeStruct((E, n1 * E, KDIM), BF16),
            jax.ShapeDtypeStruct((E, n2 * E, KDIM), BF16),
            taps(n1),
            taps(n2),
            taps(n3),
            values(n2, F32),
            values(n3, F32),
            values(n3, BF16),
            values(2, F32),
            values(len(EDGE), F32),
        ),
        in_specs=[HBM_SPEC] * 2 + [VMEM_SPEC] * 2,
        out_specs=(VMEM_SPEC,) * 14,
        scratch_shapes=[pltpu.VMEM((E, n3 * E, KDIM), BF16)]
        + [pltpu.VMEM(w1.shape, BF16)] * 2
        + [pltpu.SemaphoreType.DMA((2,))],
        compiler_params=LIMIT,
        cost_estimate=pl.CostEstimate(flops=10**9, bytes_accessed=3 << 20, transcendentals=0),
    )(w1, w2, feat, cot)


def rim_spread(first):
    lane = lax.broadcasted_iota(jnp.int32, (2 * C, 4 * C), 1)
    c = jnp.where(lane >= RIM * E, 1, 0) + jnp.where(lane >= 2 * RIM * E, 1, 0)
    cell = lane - c * (RIM * E)
    source = (cell >> 3) * RIM + (cell & (E - 1)) + c + first
    return jnp.where(lax.broadcasted_iota(jnp.int32, (2 * C, 4 * C), 0) == source, 1.0, 0.0).astype(BF16)


def fetch(pairs, sems):
    copies = [pltpu.make_async_copy(a, b, sems.at[k]) for k, (a, b) in enumerate(pairs)]
    for copy in copies:
        copy.start()
    for copy in copies:
        copy.wait()


def pack_kernel(
    even_ref,
    feat_hbm,
    cot_hbm,
    send_hbm,
    gather_hbm,
    first_ref,
    second_ref,
    codes_ref,
    feat_ref,
    cot_ref,
    send_ref,
    gather_ref,
    sems,
):
    fetch(
        (
            (feat_hbm, feat_ref),
            (cot_hbm, cot_ref),
            (send_hbm, send_ref),
            (gather_hbm, gather_ref),
        ),
        sems,
    )
    send = send_ref[...]
    upper = lax.broadcasted_iota(jnp.int32, send.shape, 1) >= FACE
    row = jnp.where(upper, send - (VOX - FACE), send)
    sent = jnp.where((row >= 0) & (row < FACE), row + 1, 0)
    slot = gather_ref[:, : 2 * C] - VOX
    bottom = jnp.where((slot >= 0) & (slot < FACE), slot + FACE + 1, 0)
    slot = gather_ref[:, -2 * C :] - (VOX + FACE)
    top = jnp.where((slot >= 0) & (slot < FACE), slot + 1, 0)

    def spread(cells, first):
        wide = jnp.broadcast_to(cells.astype(F32), (E, 2 * C)).astype(BF16)
        v = jnp.dot(wide, rim_spread(first), preferred_element_type=F32)
        return [v[:1, : 2 * C], v[:1, 2 * C :]]

    rows = [sent.astype(F32)] + spread(bottom, 0) + spread(top, 2 * C - RIM * RIM)
    codes = jnp.concatenate(rows + [jnp.zeros((E - len(rows), 2 * C), F32)], axis=0).astype(BF16)
    codes_ref[...] = codes
    even = even_ref[0] == 1

    def put(ref, upward):
        at = 0
        for source, layers in ((feat_ref, WIDE), (cot_ref, SPAN)):
            start = VOX - layers * FACE if upward else 0
            for lane in range(start, start + layers * FACE, 2 * C):
                ref[at : at + C, :] = source[0, :, lane : lane + 2 * C]
                at += C
        ref[at : at + E, :] = codes

    @pl.when(even)
    def _():
        put(first_ref, True)
        put(second_ref, False)

    @pl.when(jnp.logical_not(even))
    def _():
        put(first_ref, False)
        put(second_ref, True)


def pack(even, feat, cot, send, gather):
    rows = (WIDE + SPAN) * FACE * C // (2 * C) + E
    return pl.pallas_call(
        pack_kernel,
        out_shape=(jax.ShapeDtypeStruct((rows, 2 * C), BF16),) * 2
        + (jax.ShapeDtypeStruct((E, 2 * C), BF16),)
        + (jax.ShapeDtypeStruct(feat.shape, BF16),) * 2,
        in_specs=[SMEM_SPEC] + [HBM_SPEC] * 4,
        out_specs=(VMEM_SPEC,) * 5,
        scratch_shapes=[
            pltpu.VMEM(send.shape, jnp.int32),
            pltpu.VMEM(gather.shape, jnp.int32),
            pltpu.SemaphoreType.DMA((4,)),
        ],
        compiler_params=LIMIT,
    )(even, *(pltpu.with_memory_space_constraint(v, pltpu.HBM) for v in (feat, cot, send, gather)))


def z_shifted(v):
    axis = v.ndim - 2
    z = lax.broadcasted_iota(jnp.int32, v.shape, axis)
    before = jnp.where(z == 0, 0.0, pltpu.roll(v, 1, axis))
    after = jnp.where(z == E - 1, 0.0, pltpu.roll(v, E - 1, axis))
    return jnp.where(low_lanes(v.shape), before, v), after


def rim_cells(pick, plane):
    m = jnp.dot(pick, plane.reshape(FACE, 2 * C).astype(BF16), preferred_element_type=F32)
    m = m.reshape(3, RIM, E, 2 * C)
    return jnp.where(low_lanes(m.shape[1:]), m[0], m[1]), m[2]


def pick_matrix(send_codes, cell_codes):
    row = lax.broadcasted_iota(jnp.int32, (FACE, 2 * C), 0).astype(F32) + 1.0
    listed = jnp.where(row == send_codes, 1.0, 0.0).astype(BF16)
    slot = lax.broadcasted_iota(jnp.int32, (2 * C, 4 * C), 0).astype(F32) + 1.0
    cells = jnp.concatenate([cell_codes[0:1], cell_codes[1:2]], axis=1)
    read = jnp.where(slot == cells, 1.0, 0.0).astype(BF16)
    picked = jnp.dot(listed, read, preferred_element_type=F32)
    return jnp.transpose(picked)[:CELLS].astype(BF16)


def stack_x(planes):
    count = planes.shape[0] // E
    v = planes.reshape(count, E, E, 2 * C)
    return jnp.stack([v[:, y] for y in range(E)], axis=0)


def rounded(v):
    return v.astype(BF16).astype(F32)


def conv(q_ref, w, flipped=False):
    dims = (((1,), (0 if flipped else 1,)), ((), ()))
    step = E // SPLIT
    parts = []
    for y in range(0, E, step):
        q = q_ref[y : y + step].reshape(-1, KDIM)
        r = lax.dot_general(q, w, dims, preferred_element_type=F32)
        parts.append(r.reshape(step, -1, E, 4 * C))
    return jnp.concatenate(parts, axis=0)


def x_taps(banks, planes):
    def taps(names, lanes):
        parts = []
        for name in names:
            for r, held in banks:
                if name in held:
                    k = held.index(name)
                    parts.append(r[:, k : k + 1, :, lanes])
        return jnp.concatenate(parts, axis=1)

    low, high = slice(0, 2 * C), slice(2 * C, 4 * C)
    prev = taps([(side, x - 1) for side, x in planes], low)
    here = taps(planes, low)
    after = taps([(side, x + 1) for side, x in planes], high)
    s = jnp.where(low_lanes(here.shape), prev, here)
    return s + pltpu.roll(s, C, 3) + after


def planes_of(t):
    return stack_x(jnp.transpose(jnp.concatenate([t, t], axis=0)).reshape(-1, E, 2 * C))


def put_rows(out_ref, v):
    rows = jnp.stack([v[:, x] for x in range(E)], axis=0).reshape(VOX, 2 * C)
    out_ref[0] = jnp.transpose(rows)[:C].astype(BF16)


def put_interior(q_ref, first, v):
    count = v.shape[1]
    rows = pl.ds(first * E, count * E)
    z0, z1 = z_shifted(v)
    z0 = z0.reshape(E, count * E, 2 * C).astype(BF16)
    zero = jnp.zeros((1, count, E, 2 * C), F32)
    pair = jnp.where(low_lanes(v.shape), jnp.concatenate([zero, z1[: E - 1]], axis=0), z1)
    pair = pair.reshape(E, count * E, 2 * C).astype(BF16)
    z1 = z1.reshape(E, count * E, 2 * C).astype(BF16)
    none = jnp.zeros((count * E, 2 * C), BF16)
    for y in range(E):
        q_ref[y, rows, 0 : 2 * C] = z0[y - 1] if y > 0 else none
        q_ref[y, rows, 2 * C : 4 * C] = z0[y]
        q_ref[y, rows, 4 * C : 6 * C] = z0[y + 1] if y < E - 1 else none
        q_ref[y, rows, 6 * C : 8 * C] = pair[y]
        q_ref[y, rows, 8 * C : 10 * C] = z1[y + 1] if y < E - 1 else none


def put_rims(q_ref, first, rims):
    count = len(rims)
    rows = pl.ds(first * E, count * E)
    z0 = jnp.stack([r[0] for r in rims], axis=1)
    z1 = jnp.stack([r[1] for r in rims], axis=1)
    pair = jnp.where(low_lanes(z1[:-1].shape), z1[:-1], z1[1:])
    z0 = z0.reshape(RIM, count * E, 2 * C).astype(BF16)
    z1 = z1.reshape(RIM, count * E, 2 * C).astype(BF16)
    pair = pair.reshape(RIM - 1, count * E, 2 * C).astype(BF16)
    for y in range(E):
        for b in range(3):
            q_ref[y, rows, b * 2 * C : (b + 1) * 2 * C] = z0[y + b]
        q_ref[y, rows, 6 * C : 8 * C] = pair[y]
        q_ref[y, rows, 8 * C : 10 * C] = z1[y + 2]


def put_seams(q_ref, first, low, ends, high, picks):
    low_pick, below_pick, above_pick, high_pick = picks
    rims = (
        rim_cells(low_pick, ends[:, 0]),
        rim_cells(high_pick, ends[:, 1]),
        rim_cells(below_pick, low[:, -1]),
        rim_cells(above_pick, high[:, 0]),
    )
    put_rims(q_ref, first, rims)


def put_outer(q_ref, low, ends, high, picks, count):
    n = low.shape[1]
    mixed = []
    for k in range(n):
        mixed += [low[:, k : k + 1], high[:, n - 1 - k : n - k]]
    put_interior(q_ref, 0, jnp.concatenate(mixed, axis=1))
    put_seams(q_ref, 2 * n, low, ends, high, picks)
    put_interior(q_ref, 2 * n + len(SEAMS), ends[:, :count])


def main_kernel(
    flags_ref,
    ends_ref,
    edge_ref,
    first_ref,
    second_ref,
    codes_ref,
    f1_ref,
    f2_ref,
    b2_ref,
    q1_ref,
    q2_ref,
    r1_ref,
    r2_ref,
    r3_ref,
    slope_ref,
    inner_delta_ref,
    out_ref,
    grad_ref,
    delta_ref,
    pick_ref,
    next_ref,
    seam_ref,
    o2_ref,
    o3_ref,
):
    flags = flags_ref[0]
    even, has_lower, has_upper = ((flags & bit) > 0 for bit in (1, 2, 4))
    first = first_ref[...]
    second = second_ref[...]
    upper = jnp.where(has_upper, jnp.where(even, first, second).astype(F32), 0.0)
    lower = jnp.where(has_lower, jnp.where(even, second, first).astype(F32), 0.0)

    def parts(packed):
        blocks = [packed[k * C : (k + 1) * C] for k in range((WIDE + SPAN) // 2)]
        codes = packed[len(blocks) * C :]
        f = jnp.concatenate(blocks[: WIDE // 2], axis=1)
        c = jnp.concatenate(blocks[WIDE // 2 :], axis=1)
        return planes_of(f), planes_of(c), codes

    low_f, low_c, low_codes = parts(lower)
    high_f, high_c, high_codes = parts(upper)
    codes = codes_ref[...].astype(F32)

    def order(v, *names):
        return jnp.concatenate([v[:, EDGE.index(n) : EDGE.index(n) + 1] for n in names], axis=1)

    picks = (
        pick_matrix(codes[0:1], low_codes[3:5]),
        pick_matrix(low_codes[0:1], codes[1:3]),
        pick_matrix(high_codes[0:1], codes[3:5]),
        pick_matrix(codes[0:1], high_codes[1:3]),
    )
    pick_ref[0] = picks[1]
    pick_ref[1] = picks[2]

    def weight_gradient(which, banks, delta):
        def plane(x):
            return delta[:, x : x + 1] if 0 <= x < E else jnp.zeros((E, 1, E, 2 * C), F32)

        g = 0.0
        for q, names in banks:
            rows = E * len(names) * E
            up, here, down = (
                jnp.concatenate([plane(x + k) for _, x in names], axis=1) for k in (1, 0, -1)
            )
            d0 = jnp.where(low_lanes(here.shape), up, here)
            d0 = jnp.transpose(d0.reshape(rows, 2 * C)).astype(BF16)
            d1 = jnp.transpose(down.reshape(rows, 2 * C))[:C].astype(BF16)
            d = jnp.concatenate([d0, d1], axis=0)
            g += jnp.dot(d, q.reshape(rows, KDIM), preferred_element_type=F32)
        rows = 3 * C
        for t in range(TILES - 1):
            grad_ref[which, t * rows : (t + 1) * rows, :] = g[:, t * 2 * C : (t + 1) * 2 * C].astype(BF16)
        last = g[:, (TILES - 1) * 2 * C :]
        packed = jnp.where(
            low_lanes((rows // 2, 2 * C)), last[: rows // 2], pltpu.roll(last[rows // 2 :], C, 1)
        )
        grad_ref[which, (TILES - 1) * rows :, :] = packed.astype(BF16)

    def near(side, count):
        return tuple((-1, E - count + k) if side < 0 else (1, k) for k in range(count))

    def from_plane(ref, names, first):
        return ref[:, first * E :, :], names[first:]

    put_interior(next_ref, 0, jnp.concatenate([low_f, high_f], axis=1))
    put_seams(seam_ref, 0, low_f, ends_ref[...], high_f, picks)
    r_next = conv(next_ref, f1_ref[...])
    banks = (
        (r1_ref[...], INNER1),
        (r_next, near(-1, WIDE) + near(1, WIDE)),
        (conv(seam_ref, f1_ref[...]), SEAMS),
    )
    pre_low, pre_ends, pre_high = (
        x_taps(banks, p) for p in (near(-1, WIDE - 1), (OWN[0], OWN[-1]), near(1, WIDE - 1))
    )
    act_low, act_ends, act_high = (rounded(v * sigmoid(v)) for v in (pre_low, pre_ends, pre_high))
    put_outer(o2_ref, act_low, act_ends, act_high, picks, 2)
    banks = ((r2_ref[...], INNER2), (conv(o2_ref, f2_ref[...]), OUTER2))
    pre_edge = x_taps(banks, EDGE)
    out_ref[...] = (pre_edge * sigmoid(pre_edge)).astype(BF16)
    delta_edge = rounded(edge_ref[...] * slope(pre_edge))
    delta_low = rounded(low_c * slope(x_taps(banks, near(-1, SPAN))))
    delta_high = rounded(high_c * slope(x_taps(banks, near(1, SPAN))))
    put_outer(o3_ref, delta_low, order(delta_edge, OWN[0], OWN[-1], OWN[1], OWN[-2]), delta_high, picks, 4)
    banks = ((r3_ref[...], INNER3), (conv(o3_ref, b2_ref[...], True), OUTER3))
    delta_own = jnp.concatenate([delta_edge[:, :2], inner_delta_ref[...], delta_edge[:, 2:]], axis=1)
    beside = len(OUTER2) - 4
    weight_gradient(1, ((q2_ref[...], INNER2), from_plane(o2_ref, OUTER2, beside)), delta_own)
    slope_ends = slope(pre_ends)
    slopes = jnp.concatenate([slope_ends[:, :1], slope_ref[...], slope_ends[:, 1:]], axis=1)
    first_own = rounded(x_taps(banks, OWN) * slopes)
    first_low = rounded(x_taps(banks, near(-1, 1)) * slope(pre_low[:, -1:]))
    first_high = rounded(x_taps(banks, near(1, 1)) * slope(pre_high[:, :1]))
    delta = jnp.concatenate([first_low, first_own, first_high], axis=1)
    delta_ref[...] = delta.reshape(E, (E + 2) * E, 2 * C).astype(BF16)
    weight_gradient(0, ((q1_ref[...], INNER1), from_plane(seam_ref, SEAMS, 2)), first_own)


def main_call(*operands):
    outer = [pltpu.VMEM((E, len(names) * E, KDIM), BF16) for names in (beyond(0), SEAMS, OUTER2, OUTER3)]
    return pl.pallas_call(
        main_kernel,
        out_shape=(
            jax.ShapeDtypeStruct((E, len(EDGE), E, 2 * C), BF16),
            jax.ShapeDtypeStruct((2, 27 * C // 2, 2 * C), BF16),
            jax.ShapeDtypeStruct((E, (E + 2) * E, 2 * C), BF16),
            jax.ShapeDtypeStruct((2, CELLS, FACE), BF16),
        ),
        in_specs=[SMEM_SPEC] + [VMEM_SPEC] * (len(operands) - 1),
        out_specs=(VMEM_SPEC,) * 4,
        scratch_shapes=outer,
        compiler_params=LIMIT,
        cost_estimate=pl.CostEstimate(flops=10**10, bytes_accessed=4 << 20, transcendentals=10**6),
    )(*operands)


def last_kernel(edge_ref, inner_ref, delta_ref, pick_ref, b1_ref, out_ref, grad_ref, q_ref, rim_ref):
    edge = edge_ref[...].astype(F32)
    put_rows(out_ref, jnp.concatenate([edge[:, :2], inner_ref[...].astype(F32), edge[:, 2:]], axis=1))
    delta = delta_ref[...].astype(F32).reshape(E, E + 2, E, 2 * C)
    put_interior(q_ref, 0, delta[:, 1 : E + 1])
    put_rims(rim_ref, 0, (rim_cells(pick_ref[0], delta[:, 0]), rim_cells(pick_ref[1], delta[:, E + 1])))
    banks = ((conv(q_ref, b1_ref[...], True), OWN), (conv(rim_ref, b1_ref[...], True), SEAMS[2:]))
    put_rows(grad_ref, x_taps(banks, OWN))


def last_call(edge, inner, delta, pick, b1, shape):
    return pl.pallas_call(
        last_kernel,
        out_shape=(jax.ShapeDtypeStruct(shape, BF16),) * 2,
        in_specs=[VMEM_SPEC] * 5,
        out_specs=(VMEM_SPEC,) * 2,
        scratch_shapes=[pltpu.VMEM((E, FACE, KDIM), BF16), pltpu.VMEM((E, 2 * E, KDIM), BF16)],
        compiler_params=LIMIT,
        cost_estimate=pl.CostEstimate(flops=10**9, bytes_accessed=2 << 20, transcendentals=0),
    )(edge, inner, delta, pick, b1)


def unpack(packed, scale, out_ref):
    rows = 3 * C
    v = packed.astype(F32) * scale
    last = v[(TILES - 1) * rows :]
    last = jnp.concatenate([last[:, :C], last[:, C:]], axis=0)
    tiles = [v[t * rows : (t + 1) * rows] for t in range(TILES - 1)] + [last]
    for a in range(3):
        at = {}
        for t, pair in enumerate(PAIRS):
            for h, bc in enumerate(pair):
                if bc is not None:
                    at[3 * bc[0] + bc[1]] = tiles[t][a * C : (a + 1) * C, h * C : (h + 1) * C]
        out_ref[:, 9 * a * C : 9 * (a + 1) * C] = jnp.concatenate([at[o] for o in range(9)], axis=1)


def half_call(mine, scale):
    def kernel(mine_ref, out_ref):
        unpack(mine_ref[...], scale, out_ref)

    return pl.pallas_call(
        kernel,
        out_shape=jax.ShapeDtypeStruct((C, 27 * C), F32),
        in_specs=[VMEM_SPEC],
        out_specs=VMEM_SPEC,
        compiler_params=LIMIT,
        cost_estimate=pl.CostEstimate(flops=0, bytes_accessed=1 << 20, transcendentals=0),
    )(mine)


def finish_kernel(scale, flag_ref, mine_ref, theirs_ref, g1_hbm, g2_hbm, other_ref, sems):
    swapped = flag_ref[0] == 1

    def put(mine_hbm, other_hbm):
        first = pltpu.make_async_copy(mine_ref, mine_hbm, sems.at[0])
        first.start()
        unpack(theirs_ref[...], scale, other_ref)
        second = pltpu.make_async_copy(other_ref, other_hbm, sems.at[1])
        second.start()
        first.wait()
        second.wait()

    @pl.when(swapped)
    def _():
        put(g2_hbm, g1_hbm)

    @pl.when(jnp.logical_not(swapped))
    def _():
        put(g1_hbm, g2_hbm)


def finish(flag, mine, theirs, scale):
    shape = jax.ShapeDtypeStruct((C, 27 * C), F32)
    return pl.pallas_call(
        lambda *refs: finish_kernel(scale, *refs),
        out_shape=(shape, shape),
        in_specs=[SMEM_SPEC] + [VMEM_SPEC] * 2,
        out_specs=(HBM_SPEC,) * 2,
        scratch_shapes=[pltpu.VMEM((C, 27 * C), F32), pltpu.SemaphoreType.DMA((2,))],
        compiler_params=LIMIT,
    )(flag, mine, theirs)


HALO_ORDER = (0, 0)
PLANE_ORDER = ((3, 2, 1), (3, 1, 2))
COLUMN_ORDER = ((3, 2, 1), (3, 1, 2))


def xor_permute(v, bits):
    bricks = lax.axis_size("brick")
    pairs = []
    for i in range(lax.axis_size("scene") * bricks):
        scene, brick = i // bricks, i % bricks
        scene_bits, brick_bits = bits[scene & 1]
        pairs.append((i, (scene ^ scene_bits) * bricks + (brick ^ brick_bits)))
    return lax.ppermute(v, BOTH, pairs)


def exchange(order, core, piece, bits):
    out = []
    for ks in zip(*order):
        k = jnp.where(core == 0, ks[0], ks[1])
        out.append((k, xor_permute(piece(k), [bits(j) for j in ks])))
    return out


def all_sum(v):
    scenes, bricks = lax.axis_size("scene"), lax.axis_size("brick")
    if scenes != 4 or bricks != 8:
        total = lax.psum(v.astype(F32), BOTH)
        return jnp.zeros((1,), jnp.int32), total[0], total[1]
    scene, brick = lax.axis_index("scene"), lax.axis_index("brick")
    core, across = scene & 1, scene >> 1
    where = across * 2 + (brick & 1)
    parts = v.reshape(2, 4, -1, 2 * C)

    def pick(array, index):
        return lax.dynamic_index_in_dim(array, index, 0, keepdims=False)

    def sum4(own, arrived):
        one, two, three = (piece.astype(F32) for _, piece in arrived)
        return ((own.astype(F32) + one) + (two + three)).astype(BF16)

    def in_plane(k):
        return 2 * (k >> 1), k & 1

    def in_column(k):
        return 0, 2 * k

    core_swap = [(1, 0)] * 2
    other = xor_permute(pick(parts, 1 - core), core_swap)
    chip = (pick(parts, core).astype(F32) + other.astype(F32)).astype(BF16)
    arrived = exchange(PLANE_ORDER, core, lambda k: pick(chip, where ^ k), in_plane)
    plane = sum4(pick(chip, where), arrived)
    whole = sum4(plane, exchange(COLUMN_ORDER, core, lambda k: plane, in_column))
    arrived = exchange(PLANE_ORDER, core, lambda k: whole, in_plane)
    mine = jnp.zeros(chip.shape, BF16)
    for k, piece in [(0, whole)] + arrived:
        mine = lax.dynamic_update_index_in_dim(mine, piece, where ^ k, 0)
    mine = mine.reshape(v.shape[1:])
    theirs = xor_permute(mine, core_swap)
    return core[None], mine, theirs


def step(features, cotangent, first_weight, second_weight, send_rows, gather_rows):
    bricks = lax.axis_size("brick")
    scenes = lax.axis_size("scene")
    core = lax.axis_index("scene") & 1
    near_first = jnp.where(core == 0, HALO_ORDER[0], HALO_ORDER[1])
    even = (1 - ((lax.axis_index("brick") + near_first + 1) & 1))[None]
    brick = lax.axis_index("brick")
    flags = even + 2 * jnp.minimum(brick, 1) + 4 * jnp.minimum(bricks - 1 - brick, 1)
    feat, cot = jnp.swapaxes(features, 1, 2), jnp.swapaxes(cotangent, 1, 2)

    first, second, codes, feat, cot = pack(even, feat, cot, send_rows, gather_rows)
    within = [(i, i ^ 1) for i in range(bricks) if i ^ 1 < bricks]
    between = [(i, ((i + 1) ^ 1) - 1) for i in range(1, bricks) if ((i + 1) ^ 1) - 1 < bricks]
    turns = []
    for turn in (0, 1):
        pairs = []
        for scene in range(scenes):
            near = HALO_ORDER[scene & 1] == 1 - turn
            chosen = within if near else between
            pairs += [(scene * bricks + i, scene * bricks + j) for i, j in chosen]
            if scenes % 2 == 0:
                alone = set(range(bricks)) - {i for i, _ in chosen}
                pairs += [(scene * bricks + i, (scene ^ 1) * bricks + i) for i in sorted(alone)]
        turns.append(pairs)
    first = lax.ppermute(first, BOTH, turns[0])
    second = lax.ppermute(second, BOTH, turns[1])
    f1, f2, b1, b2, *own, inner_out, ends, edge = own_call(first_weight.T, second_weight.T, feat, cot)

    edge_out, grads, delta, pick = main_call(flags, ends, edge, first, second, codes, f1, f2, b2, *own)
    output, grad_input = last_call(edge_out, inner_out, delta, pick, b1, feat.shape)
    flag, mine, theirs = all_sum(grads)
    scale = float(lax.axis_size("scene") * bricks * VOX) ** -0.5
    mine = half_call(mine, scale)
    grad_first, grad_second = finish(flag, mine, theirs, scale)
    return jnp.swapaxes(output, 1, 2), jnp.swapaxes(grad_input, 1, 2), grad_first.T, grad_second.T


def solution(mesh):
    rows = P("scene", "brick", None)
    table = P("scene", "brick")
    return jax.shard_map(
        step,
        mesh=mesh,
        in_specs=(rows, rows, P(), P(), table, table),
        out_specs=(rows, rows, P(), P()),
        check_vma=False,
    )
```
